512 devices in a mesh: load: 16 (over x, y), gx: 8 (over z_lo, core), gy: 4 (over z_hi).
Axes of the slice: x: 4, y: 4, z: 16 (z_hi: 4, z_lo: 4; z = z_hi * 4 + z_lo), core: 2. Of those that a mesh axis runs over, the one named last changes fastest.
Arguments:
- density: float32 [64, 128, 128], P('gx', 'gy', 'load'), may hold values from 0.05 to 1
- displacement_prior: float32 [16, 3, 64, 128, 128], P('load', None, 'gx', 'gy'), may hold values from -2 to 2
- support: int32 [64, 128, 128], P('gx', 'gy'), may hold values 0 or 1
- load_nodes: int32 [16, 2048], P('load'), may hold values from 0 to 1048575
- load_forces: float32 [16, 3, 2048], P('load'), may hold values from -6 to 6
Outputs:
- displacement: float32 [16, 3, 64, 128, 128], P('load', None, 'gx', 'gy')
- filtered_sensitivity: float32 [64, 128, 128], P('gx', 'gy', 'load')
The draws below stay inside these ranges and needn't reach their ends.
Inputs may be any that keep to these rules, and one draw needn't show every extreme that they name: `load_nodes`: A node may be named several times; its forces add.
All inputs are finite; a program needn't handle non-finite values. No bound on the sum of `support` on one device may be relied on, other than what follows from the above.
Results may differ from the reference program's by a relative error of at most 0.0001.
Values sent between devices are 32-bit elements; how exact they have to be, the bound alone decides.
A program may use at most 64 MiB of HBM per device.

```python
import math
import jax
import jax.numpy as jnp
import numpy as np
from jax import lax

SWEEPS = 4
JACOBI = 2
A = 128
B = 64
C = 128
LOADS = 16
PICKS = 2048


def with_ends(values, key, low, high):
    dims = values.shape
    place = [jax.random.randint(jax.random.fold_in(key, axis), (), 0, dims[axis]) for axis in range(len(dims))]
    values = values.at[tuple(place)].set(low)
    longest = dims.index(max(dims))
    place[longest] = (place[longest] + 1) % dims[longest]
    return values.at[tuple(place)].set(high)


def block_scale(stream_key, shape, split, least, top_value):
    level = 1.0
    for axis_at, shards_of in split:
        draws = jax.random.uniform(jax.random.fold_in(jax.random.fold_in(stream_key, 6), axis_at), (shards_of,), jnp.float32, least / len(split), top_value / len(split))
        level = level * jnp.repeat(jnp.exp(draws), shape[axis_at] // shards_of).reshape((-1,) + (1,) * (len(shape) - 1 - axis_at))
    return level


def normal_values(stream_key, dims, spread, reach, split=(), held_as=jnp.bfloat16):
    gain = block_scale(stream_key, dims, split, -0.22, 0.18) if split else 1.0
    array = jax.random.normal(stream_key, dims, jnp.float32) * spread * gain
    return jnp.minimum(jnp.maximum(array, -reach), reach).astype(held_as)


def setup_inputs(seed: int = 0) -> dict:
    splits = jax.random.split(jax.random.key(seed), 6)
    density = jnp.clip(jnp.exp(math.log(1.0) - 2.9957323 * jax.random.uniform(splits[0], (B, C, A), jnp.float32) ** block_scale(splits[0], (B, C, A), ((0, 8), (1, 4), (2, 16)), -0.2, 0.2)), 0.05, 1.0)
    displacement_prior = normal_values(splits[1], (LOADS, 3, B, C, A), 0.3, 2.0, ((0, 16), (2, 8), (3, 4)), jnp.float32)
    support = with_ends((jax.random.randint(splits[2], (B, C, A), 0, 8) < 1).astype(jnp.int32), jax.random.fold_in(splits[2], 1), 0, 1)
    load_nodes = with_ends(jax.random.randint(splits[3], (LOADS, PICKS), 0, A * B * C), jax.random.fold_in(splits[3], 1), 0, (A * B * C) - 1).astype(jnp.int32)
    load_forces = normal_values(splits[4], (LOADS, 3, PICKS), 1.0, 6.0, ((0, 16),), jnp.float32)
    return dict(density=density, displacement_prior=displacement_prior, support=support, load_nodes=load_nodes, load_forces=load_forces)


poisson_ratio = 0.3
filter_weight = 3.0
relax_factor = 0.6
modulus_floor = 0.05

def element_matrix():
    lame_first = poisson_ratio / ((1 + poisson_ratio) * (1 - 2 * poisson_ratio))
    shear = 1.0 / (2 * (1 + poisson_ratio))
    elastic = np.zeros((6, 6))
    elastic[:3, :3] = lame_first
    for index in range(3):
        elastic[index, index] = lame_first + 2 * shear
        elastic[index + 3, index + 3] = shear
    points = [0.5 - 0.5 / np.sqrt(3.0), 0.5 + 0.5 / np.sqrt(3.0)]
    stiffness = np.zeros((24, 24))
    for point_x in points:
        for point_y in points:
            for point_z in points:
                strain = np.zeros((6, 24))
                for corner in range(8):
                    first, second, third = (corner & 1, corner >> 1 & 1, corner >> 2 & 1)
                    shape_x = point_x if first else 1 - point_x
                    shape_y = point_y if second else 1 - point_y
                    shape_z = point_z if third else 1 - point_z
                    slope_x = (1 if first else -1) * shape_y * shape_z
                    slope_y = shape_x * (1 if second else -1) * shape_z
                    slope_z = shape_x * shape_y * (1 if third else -1)
                    column = 3 * corner
                    strain[0, column] = slope_x
                    strain[1, column + 1] = slope_y
                    strain[2, column + 2] = slope_z
                    strain[3, column] = slope_y
                    strain[3, column + 1] = slope_x
                    strain[4, column + 1] = slope_z
                    strain[4, column + 2] = slope_y
                    strain[5, column] = slope_z
                    strain[5, column + 2] = slope_x
                stiffness = stiffness + strain.T @ elastic @ strain / 8.0
    return jnp.asarray(stiffness, dtype=jnp.float32)

def corner_bits(corner):
    return (corner & 1, corner >> 1 & 1, corner >> 2 & 1)

def corner_values(nodes, extent):
    pieces = []
    for corner in range(8):
        first, second, third = corner_bits(corner)
        pieces.append(nodes[:, first:first + extent[0], second:second + extent[1], third:third + extent[2]])
    return jnp.concatenate(pieces, axis=0)

def assemble(forces, extent):
    total = jnp.zeros((3,) + tuple(extent), jnp.float32)
    for corner in range(8):
        first, second, third = corner_bits(corner)
        total = total + forces[3 * corner:3 * corner + 3, 1 - first:1 - first + extent[0], 1 - second:1 - second + extent[1], 1 - third:1 - third + extent[2]]
    return total

def node_diagonal(modulus_ext, diag_entries, extent):
    parts = []
    for component in range(3):
        total = jnp.zeros(tuple(extent), jnp.float32)
        for corner in range(8):
            first, second, third = corner_bits(corner)
            total = total + modulus_ext[1 - first:1 - first + extent[0], 1 - second:1 - second + extent[1], 1 - third:1 - third + extent[2]] * diag_entries[3 * corner + component]
        parts.append(total)
    return jnp.stack(parts)

def chebyshev(source):
    theta = 1.0 + 6.0 * filter_weight
    delta = 6.0 * filter_weight
    sigma = theta / delta

    def operate(field):
        padded = jnp.pad(field, 1)
        beside = padded[2:, 1:-1, 1:-1] + padded[:-2, 1:-1, 1:-1]
        beside = beside + padded[1:-1, 2:, 1:-1] + padded[1:-1, :-2, 1:-1]
        beside = beside + padded[1:-1, 1:-1, 2:] + padded[1:-1, 1:-1, :-2]
        return (1.0 + 6.0 * filter_weight) * field - filter_weight * beside
    result = jnp.zeros_like(source)
    remain = source
    direction = source / theta
    ratio = 1.0 / sigma
    for sweep in range(SWEEPS):
        result = result + direction
        remain = remain - operate(direction)
        following = 1.0 / (2.0 * sigma - ratio)
        direction = following * ratio * direction + 2.0 * following / delta * remain
        ratio = following
    return result + direction

def reference(density, displacement_prior, support, load_nodes, load_forces):
    stiff = element_matrix()
    extent = (B, C, A)
    filtered = chebyshev(density)
    modulus = modulus_floor + filtered * filtered
    modulus_ext = jnp.pad(modulus, ((1, 0), (1, 0), (1, 0)))
    free = (1 - support).astype(jnp.float32)
    diagonal = node_diagonal(modulus_ext, jnp.diagonal(stiff), extent)

    def stiffness_apply(field):
        ext = jnp.pad(field, ((0, 0), (1, 1), (1, 1), (1, 1)))
        values = corner_values(ext, (B + 1, C + 1, A + 1))
        forces = jnp.einsum('ij,jxyz->ixyz', stiff, values, precision=lax.Precision.HIGHEST) * modulus_ext[None]
        return assemble(forces, extent)

    def one_load(item):
        prior, nodes, forces = item
        flat_force = jnp.zeros((3, A * B * C), jnp.float32).at[:, nodes].add(forces)
        force = flat_force.reshape((3, B, C, A))
        field = prior
        for sweep in range(JACOBI):
            field = free * (field + relax_factor * (force - stiffness_apply(field)) / diagonal)
        ext = jnp.pad(field, ((0, 0), (0, 1), (0, 1), (0, 1)))
        values = corner_values(ext, extent)
        product = jnp.einsum('ij,jxyz->ixyz', stiff, values, precision=lax.Precision.HIGHEST)
        return (field, lax.optimization_barrier(jnp.sum(values * product, axis=0)))
    fields, energies = lax.map(one_load, (displacement_prior, load_nodes, load_forces))
    sensitivity = -(2.0 / LOADS) * filtered * lax.optimization_barrier(jnp.sum(energies, axis=0))
    return (fields, chebyshev(sensitivity))
```

```python
import functools

import jax
import jax.numpy as jnp
from jax import lax
from jax.experimental import pallas as pl
from jax.experimental.pallas import tpu as pltpu
from jax.sharding import PartitionSpec as P

SWEEPS = 4
JACOBI = 2

poisson_ratio = 0.3
filter_weight = 3.0
relax_factor = 0.6
modulus_floor = 0.05
lame = poisson_ratio / ((1 + poisson_ratio) * (1 - 2 * poisson_ratio))
shear = 1.0 / (2 * (1 + poisson_ratio))

R = 8
W = 32
A = 128
N = 3 * R * W
ROWS = 13
PITCH = 48
USED = 40
BLOCKS = USED // 8
CHUNK = 512
MESH = pl.DeviceIdType.MESH
AROUND = [(0, -1), (0, 1), (-1, -1), (-1, 1), (1, -1), (1, 1), (-1, 0), (1, 0)]


def chebyshev_factors():
    theta = 1.0 + 6.0 * filter_weight
    delta = 6.0 * filter_weight
    sigma = theta / delta
    ratio = 1.0 / sigma
    steps = []
    for _ in range(SWEEPS):
        following = 1.0 / (2.0 * sigma - ratio)
        steps.append((following * ratio, 2.0 * following / delta))
        ratio = following
    return theta, steps


def lanes(shape):
    return lax.broadcasted_iota(jnp.int32, shape, len(shape) - 1)


def lane_up(x):
    return jnp.where(lanes(x.shape) == A - 1, 0.0, pltpu.roll(x, A - 1, x.ndim - 1))


def lane_down(x):
    return jnp.where(lanes(x.shape) == 0, 0.0, pltpu.roll(x, 1, x.ndim - 1))


def turned(x, steps):
    steps %= A
    return pltpu.roll(x, steps, 1) if steps else x


def edge_pack(halves):
    lane = lanes(halves[0].shape)
    packed = jnp.zeros(halves[0].shape, jnp.float32)
    for row in range(R):
        at = W * (row % 4)
        for start, column in ((8 * row, 0), (64 + 8 * row, W - 8)):
            moved = turned(halves[row // 4], start - at - column)
            packed = jnp.where((lane >= start) & (lane < start + 8), moved, packed)
    return packed


def total(values):
    result = values[0]
    for value in values[1:]:
        result = result + value
    return result


def groups():
    return [
        ([(0, 1, 0, 0), (1, 0, 1, 0), (2, 0, 0, 1)], lame / 16, 2 * shear / 16),
        ([(0, 0, 1, 0), (1, 1, 0, 0)], shear / 16, None),
        ([(0, 0, 0, 1), (2, 1, 0, 0)], shear / 16, None),
        ([(1, 0, 0, 1), (2, 0, 1, 0)], shear / 16, None),
        ([(0, 0, 1, 1), (1, 1, 0, 1), (2, 1, 1, 0)], shear / 48, shear / 48),
        ([(0, 1, 0, 1), (1, 0, 1, 1)], lame / 48, 3 * shear / 48),
        ([(0, 1, 1, 0), (2, 0, 1, 1)], lame / 48, 3 * shear / 48),
        ([(1, 1, 1, 0), (2, 1, 0, 1)], lame / 48, 3 * shear / 48),
        ([(0, 1, 1, 1)], None, (lame + 4 * shear) / 144),
        ([(1, 1, 1, 1)], None, (lame + 4 * shear) / 144),
        ([(2, 1, 1, 1)], None, (lame + 4 * shear) / 144),
    ]


def element_forces(coefs, modulus):
    scaled = {}

    def times(weight, value):
        if weight not in scaled:
            scaled[weight] = modulus * weight
        return scaled[weight] * value

    forces = {}
    for members, joint, single in groups():
        if joint is not None:
            common = total([coefs[m] for m in members])
            if joint == single:
                for m in members:
                    forces[m] = times(joint, common + coefs[m])
                continue
            common = times(joint, common)
            for m in members:
                forces[m] = common if single is None else common + times(single, coefs[m])
        else:
            for m in members:
                forces[m] = times(single, coefs[m])
    return forces


def element_energy(coefs):
    terms = {}
    for members, joint, single in groups():
        if joint is not None:
            common = total([coefs[m] for m in members])
            terms.setdefault(joint, []).append(common * common)
        if single is not None:
            for m in members:
                terms.setdefault(single, []).append(coefs[m] * coefs[m])
    return total([weight * total(values) for weight, values in terms.items()])


def plane_sums(field, row, column):
    out = {}
    for c in range(3):
        near = field[c, row, pl.ds(column, 8), :]
        far = field[c, row, pl.ds(column + 1, 8), :]
        for q, value in ((0, near + far), (1, far - near)):
            up = lane_up(value)
            out[c, q, 0] = value + up
            out[c, q, 1] = up - value
    return out


KEYS = [(c, q, r) for c in range(3) for q in range(2) for r in range(2)]


def row_coefs(low, high):
    coefs = {}
    for c, q, r in KEYS:
        coefs[c, 0, q, r] = low[c, q, r] + high[c, q, r]
        coefs[c, 1, q, r] = high[c, q, r] - low[c, q, r]
    return coefs


def kernel(
    counts,
    depth,
    density,
    prior,
    support,
    load_nodes,
    load_forces,
    displacement,
    sensitivity,
    raw,
    own,
    tile,
    beside,
    packs,
    halo,
    halos,
    wave,
    wave2,
    remain,
    result,
    rows_low,
    rows_high,
    fixed_low,
    fixed_high,
    send_low,
    send_high,
    columns_low,
    columns_high,
    corners_low,
    corners_high,
    field,
    near_part,
    far_part,
    modulus,
    free,
    step_size,
    force,
    spread,
    energy,
    shares,
    weights,
    share,
    share_pack,
    beside2,
    packs2,
    ring_wave,
    ring_wave2,
    ring_remain,
    ring_result,
    around_send,
    around_recv,
    own_send,
    own_recv,
    halo_send,
    halo_recv,
    rows_send,
    rows_recv,
    column_send,
    column_recv,
    corner_send,
    corner_recv,
    share_send,
    share_recv,
    last_send,
    last_recv,
):
    n_load, n_x, n_y = counts
    wide = depth + 8
    load, gx, gy = lax.axis_index("load"), lax.axis_index("gx"), lax.axis_index("gy")

    def inside(dx, dy):
        return (gx + dx >= 0) & (gx + dx < n_x) & (gy + dy >= 0) & (gy + dy < n_y)

    def peer(step):
        return lax.rem(load + step, n_load)

    def each_peer(action):
        def one(step, carry):
            action(step)
            return carry

        lax.fori_loop(1, n_load, one, 0)

    def remote(src, dst, send, recv, where):
        return pltpu.make_async_remote_copy(
            src_ref=src,
            dst_ref=dst,
            send_sem=send,
            recv_sem=recv,
            device_id=where,
            device_id_type=MESH,
        )

    def toward(dx, dy):
        return (load, gx + dx, gy + dy)

    for index, (dx, dy) in enumerate(AROUND):

        @pl.when(jnp.logical_not(inside(dx, dy)))
        def _():
            if dy == 0:
                for ref in (beside, beside2):
                    ref[(dx + 1) // 2] = jnp.zeros(ref.shape[1:], jnp.float32)
            else:
                for ref in (packs, packs2):
                    ref[dx + 1, (dy + 1) // 2] = jnp.zeros(ref.shape[2:], jnp.float32)

    @pl.when(jnp.logical_not(inside(-1, 0)))
    def _():
        rows_low[...] = jnp.zeros(rows_low.shape, jnp.float32)
        fixed_low[...] = jnp.zeros(fixed_low.shape, jnp.int32)
        corners_low[0] = jnp.zeros(corners_low.shape[1:], jnp.float32)
        corners_high[0] = jnp.zeros(corners_high.shape[1:], jnp.float32)

    @pl.when(jnp.logical_not(inside(1, 0)))
    def _():
        rows_high[...] = jnp.zeros(rows_high.shape, jnp.float32)
        fixed_high[...] = jnp.zeros(fixed_high.shape, jnp.int32)
        corners_low[1] = jnp.zeros(corners_low.shape[1:], jnp.float32)
        corners_high[1] = jnp.zeros(corners_high.shape[1:], jnp.float32)

    @pl.when(jnp.logical_not(inside(0, -1)))
    def _():
        columns_low[...] = jnp.zeros(columns_low.shape, jnp.float32)

    @pl.when(jnp.logical_not(inside(0, 1)))
    def _():
        columns_high[...] = jnp.zeros(columns_high.shape, jnp.float32)

    barrier = pltpu.get_barrier_semaphore()
    each_peer(
        lambda step: pl.semaphore_signal(
            barrier, inc=1, device_id=(peer(step), gx, gy), device_id_type=MESH
        )
    )
    expected = n_load - 1
    for dx, dy in AROUND:
        expected = expected + inside(dx, dy).astype(jnp.int32)

        @pl.when(inside(dx, dy))
        def _():
            pl.semaphore_signal(
                barrier, inc=1, device_id=toward(dx, dy), device_id_type=MESH
            )

    for row in range(R):
        raw[row, :, 0:W] = density[row]
    halves = []
    for half in range(2):
        value = jnp.zeros((depth, A), jnp.float32)
        lane = lanes(value.shape)
        for row in range(4):
            moved = turned(raw[4 * half + row], W * row)
            value = jnp.where((lane >= W * row) & (lane < W * row + W), moved, value)
        halves.append(value)
        own[:, A * half : A * half + A] = value
        tile[load, :, A * half : A * half + A] = value
    own[:, 2 * A : 3 * A] = edge_pack(halves)

    for row in range(R):
        for c in range(3):
            send_low[11 * row + 3 * c : 11 * row + 3 * c + 3, :] = prior[0, c, row, 0:3, :]
            send_high[7 * row + 2 * c : 7 * row + 2 * c + 2, :] = prior[0, c, row, W - 2 : W, :]
        send_low[11 * row + 9 : 11 * row + 11, :] = support[row, 0:2, :].astype(jnp.float32)
        send_high[7 * row + 6 : 7 * row + 7, :] = support[row, W - 1 : W, :].astype(jnp.float32)

    pl.semaphore_wait(barrier, expected)

    def around(index, whole, narrow, send, recv, source, pack):
        dx, dy = AROUND[index]
        if dy == 0:
            return remote(
                source, whole.at[(1 - dx) // 2], send.at[index], recv.at[index], toward(dx, dy)
            )
        return remote(
            pack, narrow.at[1 - dx, (1 - dy) // 2], send.at[index], recv.at[index], toward(dx, dy)
        )

    first_around = [
        around(
            index,
            beside,
            packs,
            around_send,
            around_recv,
            own.at[:, pl.ds(0, 2 * A)],
            own.at[:, pl.ds(2 * A, A)],
        )
        for index in range(8)
    ]
    opposite = [AROUND.index((-dx, -dy)) for dx, dy in AROUND]

    for index, (dx, dy) in enumerate(AROUND):

        @pl.when(inside(dx, dy))
        def _():
            first_around[index].start()

    def own_copy(step):
        return remote(
            own.at[:, pl.ds(0, 2 * A)],
            tile.at[load],
            own_send.at[step],
            own_recv.at[step],
            (peer(step), gx, gy),
        )

    each_peer(lambda step: own_copy(step).start())

    row_copies = [
        (-1, remote(prior.at[0, :, pl.ds(0, 3)], rows_high, rows_send.at[0], rows_recv.at[0], toward(-1, 0))),
        (-1, remote(support.at[pl.ds(0, 2)], fixed_high, rows_send.at[1], rows_recv.at[1], toward(-1, 0))),
        (1, remote(prior.at[0, :, pl.ds(R - 2, 2)], rows_low, rows_send.at[2], rows_recv.at[2], toward(1, 0))),
        (1, remote(support.at[pl.ds(R - 1, 1)], fixed_low, rows_send.at[3], rows_recv.at[3], toward(1, 0))),
    ]
    column_copies = [
        (-1, remote(send_low, columns_high, column_send.at[0], column_recv.at[0], toward(0, -1))),
        (1, remote(send_high, columns_low, column_send.at[1], column_recv.at[1], toward(0, 1))),
    ]
    for dy, copy in column_copies:
        pl.when(inside(0, dy))(copy.start)
    for dx, copy in row_copies:
        pl.when(inside(dx, 0))(copy.start)

    flat = load_nodes[...]
    column_bits = (n_y * W).bit_length() - 1
    node_row = lax.shift_right_logical(flat, 7 + column_bits) - gx * R + 1
    node_column = (lax.shift_right_logical(flat, 7) & (n_y * W - 1)) - gy * W + 2
    held = (node_row >= 0) & (node_row < 11) & (node_column >= 0) & (node_column < USED)
    spread[0:1, :] = jnp.where(held, node_row * USED + node_column, -1)
    spread[1:2, :] = flat & (A - 1)
    force[...] = jnp.zeros(force.shape, jnp.float32)

    def add_loads(index, carry):
        span = pl.ds(pl.multiple_of(index * CHUNK, CHUNK), CHUNK)
        place = spread[0:1, span]
        depth_of = spread[1:2, span]
        left = jnp.where(
            lax.broadcasted_iota(jnp.int32, (11 * USED, CHUNK), 0) == place, 1.0, 0.0
        ).astype(jnp.bfloat16)
        here = lax.broadcasted_iota(jnp.int32, (A, CHUNK), 0) == depth_of
        rest = [load_forces[0, c : c + 1, span] for c in range(3)]
        for part in range(3):
            rights = []
            for c in range(3):
                rounded = rest[c].astype(jnp.bfloat16).astype(jnp.float32)
                rest[c] = rest[c] - rounded
                rights.append(jnp.where(here, rounded, 0.0).astype(jnp.bfloat16))
            force[...] += lax.dot_general(
                left,
                jnp.concatenate(rights, axis=0),
                (((1,), (1,)), ((), ())),
                preferred_element_type=jnp.float32,
            )
        return carry

    lax.fori_loop(0, load_nodes.shape[1] // CHUNK, add_loads, 0)

    for index, (dx, dy) in enumerate(AROUND):

        @pl.when(inside(dx, dy))
        def _():
            first_around[opposite[index]].wait_recv()

    lane = lanes((depth, A))
    halo[:, 0:A] = beside[0, :, A : 2 * A]
    halo[:, A : 2 * A] = beside[1, :, 0:A]
    halo[:, 2 * A : 3 * A] = jnp.where(lane < 64, beside[1, :, A : 2 * A], beside[0, :, 0:A])
    for index in range(3):
        at = (3 + index) * A
        halo[:, at : at + A] = jnp.where(lane < 64, packs[index, 1], packs[index, 0])
    halos[load] = halo[...]

    def halo_copy(step):
        return remote(
            halo, halos.at[load], halo_send.at[step], halo_recv.at[step], (peer(step), gx, gy)
        )

    each_peer(lambda step: halo_copy(step).start())

    for dy, copy in column_copies:
        other = column_copies[0][1] if dy == 1 else column_copies[1][1]
        pl.when(inside(0, dy))(other.wait_recv)
    corner_copies = []
    for dx in (-1, 1):
        for part, (source, target) in enumerate(
            ((columns_low, corners_low), (columns_high, corners_high))
        ):
            at = (dx + 1) + part
            corner_copies.append(
                (
                    dx,
                    remote(
                        source,
                        target.at[(1 - dx) // 2],
                        corner_send.at[at],
                        corner_recv.at[at],
                        toward(dx, 0),
                    ),
                )
            )
    for dx, copy in corner_copies:
        pl.when(inside(dx, 0))(copy.start)

    for ref in (wave, wave2, ring_wave, ring_wave2):

        def clear(row, carry):
            ref[row] = jnp.zeros(ref.shape[1:], jnp.float32)
            return carry

        lax.fori_loop(0, ref.shape[0], clear, 0)

    def clear_rows(row, carry):
        for c in range(3):
            field[c, row, W:PITCH, :] = jnp.zeros((PITCH - W, A), jnp.float32)
        free[row] = jnp.zeros((PITCH, A), jnp.float32)
        return carry

    lax.fori_loop(0, ROWS, clear_rows, 0)

    for c in range(3):
        for row in range(R):
            field[c, row + 2, 2 : 2 + W, :] = prior[0, c, row]
    for row in range(R):
        free[row + 2, 2 : 2 + W, :] = support[row].astype(jnp.float32)

    for dx, copy in row_copies + corner_copies:
        opposite_copy = {
            id(a[1]): b[1]
            for pairs in (
                (row_copies[0], row_copies[2]),
                (row_copies[1], row_copies[3]),
                (corner_copies[0], corner_copies[2]),
                (corner_copies[1], corner_copies[3]),
            )
            for a, b in (pairs, pairs[::-1])
        }[id(copy)]
        pl.when(inside(dx, 0))(opposite_copy.wait_recv)

    for c in range(3):
        for row in range(2):
            field[c, row, 2 : 2 + W, :] = rows_low[c, row]
        for row in range(3):
            field[c, row + 10, 2 : 2 + W, :] = rows_high[c, row]
    free[1, 2 : 2 + W, :] = fixed_low[0].astype(jnp.float32)
    for row in range(2):
        free[row + 10, 2 : 2 + W, :] = fixed_high[row].astype(jnp.float32)
    for row in range(-2, R + 3):
        if row < 0:
            low, high, at = corners_low.at[0], corners_high.at[0], row + R
        elif row < R:
            low, high, at = columns_low, columns_high, row
        else:
            low, high, at = corners_low.at[1], corners_high.at[1], row - R
        for c in range(3):
            field[c, row + 2, 0:2, :] = low[7 * at + 2 * c : 7 * at + 2 * c + 2, :]
            field[c, row + 2, 2 + W : 5 + W, :] = high[11 * at + 3 * c : 11 * at + 3 * c + 3, :]
        free[row + 2, 1:2, :] = low[7 * at + 6 : 7 * at + 7, :]
        free[row + 2, 2 + W : 4 + W, :] = high[11 * at + 9 : 11 * at + 11, :]

    def in_grid(row, columns):
        row, columns = row + gx * R, columns + gy * W
        return (row >= 0) & (row < n_x * R) & (columns >= 0) & (columns < n_y * W)

    def set_free(row, carry):
        columns = lax.broadcasted_iota(jnp.int32, (PITCH, A), 0) - 2
        kept = in_grid(row - 2, columns) & (columns >= -1) & (columns <= W + 1)
        free[row] = jnp.where(kept & (free[row] == 0.0), 1.0, 0.0)
        return carry

    lax.fori_loop(1, 12, set_free, 0)

    def place(block, pieces):
        value = block.T
        for start, rows, columns, row, column in pieces:
            part = value[start : start + rows * columns].reshape(rows, columns, A)
            wave[row + 8 : row + 8 + rows, column + 16 : column + 16 + columns, :] = part

    each_peer(lambda step: own_copy(step).wait_recv())
    for half in range(2):
        place(tile[:, :, A * half : A * half + A].reshape(A, A), [(0, 4, W, 4 * half, 0)])
    each_peer(lambda step: halo_copy(step).wait_recv())
    layout = [
        [(0, 4, W, -4, 0)],
        [(0, 4, W, 8, 0)],
        [(0, 2, W, 12, 0), (64, 2, W, -6, 0)],
    ] + [[(0, 8, 8, dx * R, W), (64, 8, 8, dx * R, -8)] for dx in (-1, 0, 1)]
    for index, pieces in enumerate(layout):
        place(halos[:, :, A * index : A * index + A].reshape(A, A), pieces)

    theta, factors = chebyshev_factors()

    def start_filter(row, carry):
        source = wave[row, 8:56, :]
        direction = source / theta
        remain[row] = source
        result[row] = direction
        wave[row, 8:56, :] = direction
        return carry

    lax.fori_loop(2, 22, start_filter, 0)
    source, target = wave, wave2
    for sweep, (keep, gain) in enumerate(factors):

        def one_row(row, carry, source=source, target=target, keep=keep, gain=gain):
            middle = source[row, 8:56, :]
            near = (
                source[row - 1, 8:56, :]
                + source[row + 1, 8:56, :]
                + source[row, 7:55, :]
                + source[row, 9:57, :]
                + lane_up(middle)
                + lane_down(middle)
            )
            left = remain[row] - ((1.0 + 6.0 * filter_weight) * middle - filter_weight * near)
            columns = lax.broadcasted_iota(jnp.int32, (48, A), 0) - 8
            direction = jnp.where(in_grid(row - 8, columns), keep * middle + gain * left, 0.0)
            remain[row] = left
            result[row] = result[row] + direction
            target[row, 8:56, :] = direction
            return carry

        lax.fori_loop(3 + sweep, 21 - sweep, one_row, 0)
        source, target = target, source

    def set_modulus(row, carry):
        filtered = result[row + 6, 6 : 6 + USED, :]
        columns = lax.broadcasted_iota(jnp.int32, (USED, A), 0) - 2
        modulus[row, 0:8, :] = jnp.zeros((8, A), jnp.float32)
        modulus[row, 8 : 8 + USED, :] = jnp.where(
            in_grid(row - 2, columns), modulus_floor + filtered * filtered, 0.0
        )
        return carry

    lax.fori_loop(0, 12, set_modulus, 0)
    for half in range(2):
        tall = result[8 + 4 * half : 12 + 4 * half, 8 : 8 + W, :].reshape(A, A)
        weights[4 : 4 + A, A * half : A * half + A] = tall.T
    weights[0:4, :] = jnp.zeros((4, 2 * A), jnp.float32)
    weights[4 + A : 8 + A, :] = jnp.zeros((4, 2 * A), jnp.float32)

    def set_step(row, carry):
        around_node = total(
            [modulus[row - 1 + p, 7 + q : 7 + q + USED, :] for p in range(2) for q in range(2)]
        )
        around_node = around_node + lane_down(around_node)
        step_size[row] = relax_factor / ((lame + 4 * shear) / 9 * around_node)
        return carry

    lax.fori_loop(1, 12, set_step, 0)

    for sweep in range(JACOBI):
        first, last = 1 + sweep, 12 - sweep
        for block in range(BLOCKS):

            def one_element_row(row, carry, column=8 * block):
                low, pending = carry
                low = dict(zip(KEYS, low))
                high = plane_sums(field, row + 1, column)
                forces = element_forces(
                    row_coefs(low, high), modulus[row, pl.ds(column + 8, 8), :]
                )
                node = {}
                following = []
                for at, (c, q, r) in enumerate(KEYS):
                    change = forces[c, 1, q, r]
                    if (c, 0, q, r) in forces:
                        same = forces[c, 0, q, r]
                        node[c, q, r] = pending[at] + (same - change)
                        following.append(same + change)
                    else:
                        node[c, q, r] = pending[at] - change
                        following.append(change)
                for c in range(3):
                    both = []
                    for q in range(2):
                        lower = node[c, q, 0] - node[c, q, 1]
                        upper = node[c, q, 0] + node[c, q, 1]
                        both.append(lower + lane_down(upper))
                    near_part[c, row, pl.ds(column, 8), :] = both[0] - both[1]
                    far_part[c, row, pl.ds(column + 1, 8), :] = both[0] + both[1]
                return [high[key] for key in KEYS], following

            low = plane_sums(field, first - 1, 8 * block)
            nothing = [jnp.zeros((8, A), jnp.float32)] * len(KEYS)
            lax.fori_loop(
                first - 1, last, one_element_row, ([low[key] for key in KEYS], nothing)
            )

        def one_node_row(row, carry):
            for block in range(BLOCKS):
                span = pl.ds(8 * block, 8)
                rate = step_size[row, span, :]
                open_here = free[row, span, :] > 0.0
                for c in range(3):
                    applied = near_part[c, row, span, :] + far_part[c, row, span, :]
                    load_here = force[pl.ds(pl.multiple_of((row - 1) * USED + 8 * block, 8), 8), A * c : A * c + A]
                    moved = field[c, row, span, :] + (load_here - applied) * rate
                    field[c, row, span, :] = jnp.where(open_here, moved, 0.0)
            return carry

        lax.fori_loop(first, last, one_node_row, 0)

    for block in range(W // 8):

        def one_energy_row(row, low, column=8 * block + 2):
            high = plane_sums(field, row + 1, column)
            value = element_energy(row_coefs(dict(zip(KEYS, low)), high))
            remain[row, pl.ds(column - 2, 8), :] = value
            return [high[key] for key in KEYS]

        low = plane_sums(field, 2, 8 * block + 2)
        lax.fori_loop(2, 10, one_energy_row, [low[key] for key in KEYS])
    for half in range(2):
        tall = remain[2 + 4 * half : 6 + 4 * half, 0:W, :].reshape(A, A)
        energy[4 : 4 + A, A * half : A * half + A] = tall.T
    energy[0:4, :] = jnp.zeros((4, 2 * A), jnp.float32)
    energy[4 + A : 8 + A, :] = jnp.zeros((4, 2 * A), jnp.float32)

    for c in range(3):
        for row in range(R):
            displacement[0, c, row] = field[c, row + 2, 2 : 2 + W, :]

    def slab(owner):
        return pl.ds(pl.multiple_of(owner * depth, 8), wide)

    def share_copy(step):
        return remote(
            energy.at[slab(peer(step)), :],
            shares.at[load],
            share_send.at[step],
            share_recv.at[step],
            (peer(step), gx, gy),
        )

    each_peer(lambda step: share_copy(step).start())
    shares[load] = energy[slab(load), :]
    each_peer(lambda step: share_copy(step).wait_recv())
    summed = total([shares[index] for index in range(n_load)])
    value = -(2.0 / n_load) * weights[slab(load), :] * summed
    share[...] = value
    share_pack[...] = edge_pack([value[:, 0:A], value[:, A : 2 * A]])

    last_around = [
        around(index, beside2, packs2, last_send, last_recv, share, share_pack)
        for index in range(8)
    ]
    for index, (dx, dy) in enumerate(AROUND):

        @pl.when(inside(dx, dy))
        def _():
            last_around[index].start()

    for index, (dx, dy) in enumerate(AROUND):

        @pl.when(inside(dx, dy))
        def _():
            last_around[opposite[index]].wait_recv()

    lane = lanes((wide, A))
    for row in range(-4, R + 4):
        if row < 0:
            body, pack = beside2[0, :, A : 2 * A], 0
        elif row < R:
            body, pack = share[:, A * (row // 4) : A * (row // 4) + A], 1
        else:
            body, pack = beside2[1, :, 0:A], 2
        at = row % R
        line = turned(body, 4 - W * (at % 4))
        after = turned(packs2[pack, 1], 4 + W - 8 * at)
        before = turned(packs2[pack, 0], -4 - 64 - 8 * at)
        line = jnp.where(lane < 4, before, line)
        line = jnp.where(lane >= W + 4, after, line)
        line = jnp.where(lane < W + 8, line, 0.0)
        direction = line / theta
        ring_remain[row + 4] = line
        ring_result[row + 4] = direction
        ring_wave[row + 4, 8 : 8 + wide, :] = direction

    source, target = ring_wave, ring_wave2
    for sweep, (keep, gain) in enumerate(factors):

        def one_ring_row(row, carry, source=source, target=target, keep=keep, gain=gain):
            middle = source[row, 8 : 8 + wide, :]
            near = (
                source[row - 1, 8 : 8 + wide, :]
                + source[row + 1, 8 : 8 + wide, :]
                + source[row, 7 : 7 + wide, :]
                + source[row, 9 : 9 + wide, :]
                + pltpu.roll(middle, A - 1, 1)
                + pltpu.roll(middle, 1, 1)
            )
            left = ring_remain[row] - (
                (1.0 + 6.0 * filter_weight) * middle - filter_weight * near
            )
            layer = lax.broadcasted_iota(jnp.int32, (wide, A), 0) - 4 + load * depth
            kept = in_grid(row - 4, lane - 4) & (layer >= 0) & (layer < A) & (lane < W + 8)
            direction = jnp.where(kept, keep * middle + gain * left, 0.0)
            ring_remain[row] = left
            ring_result[row] = ring_result[row] + direction
            target[row, 8 : 8 + wide, :] = direction
            return carry

        lax.fori_loop(1 + sweep, 15 - sweep, one_ring_row, 0)
        source, target = target, source
    for row in range(R):
        moved = turned(ring_result[row + 4], -4)
        raw[row] = moved[4 : 4 + depth]
        sensitivity[row] = raw[row, :, 0:W]

    for index, (dx, dy) in enumerate(AROUND):

        @pl.when(inside(dx, dy))
        def _():
            first_around[index].wait_send()
            last_around[index].wait_send()

    for dx, copy in row_copies + corner_copies:
        pl.when(inside(dx, 0))(copy.wait_send)
    for dy, copy in column_copies:
        pl.when(inside(0, dy))(copy.wait_send)
    each_peer(lambda step: own_copy(step).wait_send())
    each_peer(lambda step: halo_copy(step).wait_send())
    each_peer(lambda step: share_copy(step).wait_send())


def body(counts, density, displacement_prior, support, load_nodes, load_forces):
    n_load = counts[0]
    depth = A // n_load
    wide = depth + 8
    picks = load_nodes.shape[1]
    real, whole = jnp.float32, jnp.int32
    scratch = [
        ((R, depth, A), real),
        ((depth, 3 * A), real),
        ((n_load, depth, 2 * A), real),
        ((2, depth, 2 * A), real),
        ((3, 2, depth, A), real),
        ((depth, 6 * A), real),
        ((n_load, depth, 6 * A), real),
        ((24, 64, A), real),
        ((24, 64, A), real),
        ((24, 48, A), real),
        ((24, 48, A), real),
        ((3, 2, W, A), real),
        ((3, 3, W, A), real),
        ((1, W, A), whole),
        ((2, W, A), whole),
        ((11 * R, A), real),
        ((7 * R, A), real),
        ((7 * R, A), real),
        ((11 * R, A), real),
        ((2, 7 * R, A), real),
        ((2, 11 * R, A), real),
        ((3, ROWS, PITCH, A), real),
        ((3, ROWS, PITCH, A), real),
        ((3, ROWS, PITCH, A), real),
        ((12, 8 + USED, A), real),
        ((ROWS, PITCH, A), real),
        ((12, USED, A), real),
        ((11 * USED, 3 * A), real),
        ((8, picks), whole),
        ((A + 8, 2 * A), real),
        ((n_load, wide, 2 * A), real),
        ((A + 8, 2 * A), real),
        ((wide, 2 * A), real),
        ((wide, A), real),
        ((2, wide, 2 * A), real),
        ((3, 2, wide, A), real),
        ((16, wide + 16, A), real),
        ((16, wide + 16, A), real),
        ((16, wide, A), real),
        ((16, wide, A), real),
    ]
    semaphores = [8, 8, n_load, n_load, n_load, n_load, 4, 4, 2, 2, 4, 4, n_load, n_load, 8, 8]
    displacement, sensitivity = pl.pallas_call(
        functools.partial(kernel, counts, depth),
        out_shape=(
            jax.ShapeDtypeStruct(displacement_prior.shape, real),
            jax.ShapeDtypeStruct((R, depth, W), real),
        ),
        in_specs=[pl.BlockSpec(memory_space=pltpu.VMEM)] * 5,
        out_specs=(pl.BlockSpec(memory_space=pltpu.VMEM),) * 2,
        scratch_shapes=[pltpu.VMEM(shape, kind) for shape, kind in scratch]
        + [pltpu.SemaphoreType.DMA((count,)) for count in semaphores],
        compiler_params=pltpu.CompilerParams(
            collective_id=0, has_side_effects=True, vmem_limit_bytes=48 << 20
        ),
        name="elasticity",
    )(
        jnp.transpose(density, (0, 2, 1)),
        displacement_prior,
        support,
        load_nodes,
        load_forces,
    )
    return displacement, jnp.transpose(sensitivity, (0, 2, 1))


def solution(mesh):
    counts = tuple(mesh.shape[axis] for axis in ("load", "gx", "gy"))
    return jax.shard_map(
        functools.partial(body, counts),
        mesh=mesh,
        in_specs=(
            P("gx", "gy", "load"),
            P("load", None, "gx", "gy", None),
            P("gx", "gy", None),
            P("load", None),
            P("load", None, None),
        ),
        out_specs=(P("load", None, "gx", "gy", None), P("gx", "gy", "load")),
        check_vma=False,
    )
```

```python
import functools

import jax
import jax.numpy as jnp
from jax import lax
from jax.experimental import pallas as pl
from jax.experimental.pallas import tpu as pltpu
from jax.sharding import PartitionSpec as P

SWEEPS = 4
JACOBI = 2

poisson_ratio = 0.3
filter_weight = 3.0
relax_factor = 0.6
modulus_floor = 0.05
lame = poisson_ratio / ((1 + poisson_ratio) * (1 - 2 * poisson_ratio))
shear = 1.0 / (2 * (1 + poisson_ratio))

R = 8
W = 32
A = 128
N = 3 * R * W
ROWS = 13
PITCH = 48
USED = 40
BLOCKS = USED // 8
CHUNK = 512
MESH = pl.DeviceIdType.MESH
AROUND = [(0, -1), (0, 1), (-1, -1), (-1, 1), (1, -1), (1, 1), (-1, 0), (1, 0)]


def chebyshev_factors():
    theta = 1.0 + 6.0 * filter_weight
    delta = 6.0 * filter_weight
    sigma = theta / delta
    ratio = 1.0 / sigma
    steps = []
    for _ in range(SWEEPS):
        following = 1.0 / (2.0 * sigma - ratio)
        steps.append((following * ratio, 2.0 * following / delta))
        ratio = following
    return theta, steps


def lanes(shape):
    return lax.broadcasted_iota(jnp.int32, shape, len(shape) - 1)


def lane_up(x):
    return jnp.where(lanes(x.shape) == A - 1, 0.0, pltpu.roll(x, A - 1, x.ndim - 1))


def lane_down(x):
    return jnp.where(lanes(x.shape) == 0, 0.0, pltpu.roll(x, 1, x.ndim - 1))


def turned(x, steps):
    steps %= A
    return pltpu.roll(x, steps, 1) if steps else x


def edge_pack(halves):
    lane = lanes(halves[0].shape)
    packed = jnp.zeros(halves[0].shape, jnp.float32)
    for row in range(R):
        at = W * (row % 4)
        for start, column in ((8 * row, 0), (64 + 8 * row, W - 8)):
            moved = turned(halves[row // 4], start - at - column)
            packed = jnp.where((lane >= start) & (lane < start + 8), moved, packed)
    return packed


def total(values):
    result = values[0]
    for value in values[1:]:
        result = result + value
    return result


def groups():
    return [
        ([(0, 1, 0, 0), (1, 0, 1, 0), (2, 0, 0, 1)], lame / 16, 2 * shear / 16),
        ([(0, 0, 1, 0), (1, 1, 0, 0)], shear / 16, None),
        ([(0, 0, 0, 1), (2, 1, 0, 0)], shear / 16, None),
        ([(1, 0, 0, 1), (2, 0, 1, 0)], shear / 16, None),
        ([(0, 0, 1, 1), (1, 1, 0, 1), (2, 1, 1, 0)], shear / 48, shear / 48),
        ([(0, 1, 0, 1), (1, 0, 1, 1)], lame / 48, 3 * shear / 48),
        ([(0, 1, 1, 0), (2, 0, 1, 1)], lame / 48, 3 * shear / 48),
        ([(1, 1, 1, 0), (2, 1, 0, 1)], lame / 48, 3 * shear / 48),
        ([(0, 1, 1, 1)], None, (lame + 4 * shear) / 144),
        ([(1, 1, 1, 1)], None, (lame + 4 * shear) / 144),
        ([(2, 1, 1, 1)], None, (lame + 4 * shear) / 144),
    ]


def element_forces(coefs, modulus):
    scaled = {}

    def times(weight, value):
        if weight not in scaled:
            scaled[weight] = modulus * weight
        return scaled[weight] * value

    forces = {}
    for members, joint, single in groups():
        if joint is not None:
            common = total([coefs[m] for m in members])
            if joint == single:
                for m in members:
                    forces[m] = times(joint, common + coefs[m])
                continue
            common = times(joint, common)
            for m in members:
                forces[m] = common if single is None else common + times(single, coefs[m])
        else:
            for m in members:
                forces[m] = times(single, coefs[m])
    return forces


def element_energy(coefs):
    terms = {}
    for members, joint, single in groups():
        if joint is not None:
            common = total([coefs[m] for m in members])
            terms.setdefault(joint, []).append(common * common)
        if single is not None:
            for m in members:
                terms.setdefault(single, []).append(coefs[m] * coefs[m])
    return total([weight * total(values) for weight, values in terms.items()])


def plane_sums(field, lifted, row, column):
    out = {}
    for c in range(3):
        near = field[c, row, pl.ds(column, 8), :]
        far = field[c, row, pl.ds(column + 1, 8), :]
        near_up = lifted[c, row, pl.ds(column, 8), :]
        far_up = lifted[c, row, pl.ds(column + 1, 8), :]
        for q, value, up in ((0, near + far, near_up + far_up), (1, far - near, far_up - near_up)):
            out[c, q, 0] = value + up
            out[c, q, 1] = up - value
    return out


def in_groups(first, last, size, action, carry=0):
    trips = (last - first) // size

    def trip(index, carry):
        for at in range(size):
            carry = action(first + index * size + at, carry)
        return carry

    if trips > 1:
        carry = lax.fori_loop(0, trips, trip, carry)
        first += trips * size
    for row in range(first, last):
        carry = action(row, carry)
    return carry


KEYS = [(c, q, r) for c in range(3) for q in range(2) for r in range(2)]


def row_coefs(low, high):
    coefs = {}
    for c, q, r in KEYS:
        coefs[c, 0, q, r] = low[c, q, r] + high[c, q, r]
        coefs[c, 1, q, r] = high[c, q, r] - low[c, q, r]
    return coefs


def kernel(
    counts,
    depth,
    density_in,
    prior_in,
    support_in,
    nodes_in,
    forces_in,
    displacement,
    sensitivity,
    density,
    prior,
    support,
    load_nodes,
    load_forces,
    raw,
    own,
    tile,
    beside,
    packs,
    halo,
    halos,
    wave,
    wave2,
    remain,
    result,
    rows_low,
    rows_high,
    fixed_low,
    fixed_high,
    send_low,
    send_high,
    columns_low,
    columns_high,
    corners_low,
    corners_high,
    field,
    near_part,
    far_part,
    modulus,
    free,
    step_size,
    force,
    spread,
    energy,
    shares,
    weights,
    share,
    share_pack,
    beside2,
    packs2,
    ring_wave,
    ring_wave2,
    ring_remain,
    ring_result,
    lifted,
    near_upper,
    far_upper,
    mask,
    ring_mask,
    around_send,
    around_recv,
    own_send,
    own_recv,
    halo_send,
    halo_recv,
    rows_send,
    rows_recv,
    column_send,
    column_recv,
    corner_send,
    corner_recv,
    share_send,
    share_recv,
    last_send,
    last_recv,
    fetched,
):
    n_load, n_x, n_y = counts
    wide = depth + 8
    load, gx, gy = lax.axis_index("load"), lax.axis_index("gx"), lax.axis_index("gy")

    def inside(dx, dy):
        return (gx + dx >= 0) & (gx + dx < n_x) & (gy + dy >= 0) & (gy + dy < n_y)

    def peer(step):
        return lax.rem(load + step, n_load)

    def each_peer(action):
        def one(step, carry):
            action(step)
            return carry

        lax.fori_loop(1, n_load, one, 0)

    def remote(src, dst, send, recv, where):
        return pltpu.make_async_remote_copy(
            src_ref=src,
            dst_ref=dst,
            send_sem=send,
            recv_sem=recv,
            device_id=where,
            device_id_type=MESH,
        )

    def toward(dx, dy):
        return (load, gx + dx, gy + dy)

    fetches = [
        pltpu.make_async_copy(source, target, fetched.at[index])
        for index, (source, target) in enumerate(
            (
                (density_in, density),
                (prior_in, prior),
                (support_in, support),
                (nodes_in, load_nodes),
                (forces_in, load_forces),
            )
        )
    ]
    for fetch in fetches:
        fetch.start()

    for index, (dx, dy) in enumerate(AROUND):

        @pl.when(jnp.logical_not(inside(dx, dy)))
        def _():
            if dy == 0:
                for ref in (beside, beside2):
                    ref[(dx + 1) // 2] = jnp.zeros(ref.shape[1:], jnp.float32)
            else:
                for ref in (packs, packs2):
                    ref[dx + 1, (dy + 1) // 2] = jnp.zeros(ref.shape[2:], jnp.float32)

    @pl.when(jnp.logical_not(inside(-1, 0)))
    def _():
        rows_low[...] = jnp.zeros(rows_low.shape, jnp.float32)
        fixed_low[...] = jnp.zeros(fixed_low.shape, jnp.int32)
        corners_low[0] = jnp.zeros(corners_low.shape[1:], jnp.float32)
        corners_high[0] = jnp.zeros(corners_high.shape[1:], jnp.float32)

    @pl.when(jnp.logical_not(inside(1, 0)))
    def _():
        rows_high[...] = jnp.zeros(rows_high.shape, jnp.float32)
        fixed_high[...] = jnp.zeros(fixed_high.shape, jnp.int32)
        corners_low[1] = jnp.zeros(corners_low.shape[1:], jnp.float32)
        corners_high[1] = jnp.zeros(corners_high.shape[1:], jnp.float32)

    @pl.when(jnp.logical_not(inside(0, -1)))
    def _():
        columns_low[...] = jnp.zeros(columns_low.shape, jnp.float32)

    @pl.when(jnp.logical_not(inside(0, 1)))
    def _():
        columns_high[...] = jnp.zeros(columns_high.shape, jnp.float32)

    barrier = pltpu.get_barrier_semaphore()
    each_peer(
        lambda step: pl.semaphore_signal(
            barrier, inc=1, device_id=(peer(step), gx, gy), device_id_type=MESH
        )
    )
    expected = n_load - 1
    for dx, dy in AROUND:
        expected = expected + inside(dx, dy).astype(jnp.int32)

        @pl.when(inside(dx, dy))
        def _():
            pl.semaphore_signal(
                barrier, inc=1, device_id=toward(dx, dy), device_id_type=MESH
            )

    fetches[0].wait()
    for row in range(R):
        raw[row, :, 0:W] = density[row]
    halves = []
    for half in range(2):
        value = jnp.zeros((depth, A), jnp.float32)
        lane = lanes(value.shape)
        for row in range(4):
            moved = turned(raw[4 * half + row], W * row)
            value = jnp.where((lane >= W * row) & (lane < W * row + W), moved, value)
        halves.append(value)
        own[:, A * half : A * half + A] = value
        tile[load, :, A * half : A * half + A] = value
    own[:, 2 * A : 3 * A] = edge_pack(halves)

    fetches[1].wait()
    fetches[2].wait()

    for row in range(R):
        for c in range(3):
            send_low[11 * row + 3 * c : 11 * row + 3 * c + 3, :] = prior[0, c, row, 0:3, :]
            send_high[7 * row + 2 * c : 7 * row + 2 * c + 2, :] = prior[0, c, row, W - 2 : W, :]
        send_low[11 * row + 9 : 11 * row + 11, :] = support[row, 0:2, :].astype(jnp.float32)
        send_high[7 * row + 6 : 7 * row + 7, :] = support[row, W - 1 : W, :].astype(jnp.float32)

    pl.semaphore_wait(barrier, expected)

    def around(index, whole, narrow, send, recv, source, pack):
        dx, dy = AROUND[index]
        if dy == 0:
            return remote(
                source, whole.at[(1 - dx) // 2], send.at[index], recv.at[index], toward(dx, dy)
            )
        return remote(
            pack, narrow.at[1 - dx, (1 - dy) // 2], send.at[index], recv.at[index], toward(dx, dy)
        )

    first_around = [
        around(
            index,
            beside,
            packs,
            around_send,
            around_recv,
            own.at[:, pl.ds(0, 2 * A)],
            own.at[:, pl.ds(2 * A, A)],
        )
        for index in range(8)
    ]
    opposite = [AROUND.index((-dx, -dy)) for dx, dy in AROUND]

    for index, (dx, dy) in enumerate(AROUND):

        @pl.when(inside(dx, dy))
        def _():
            first_around[index].start()

    def own_copy(step):
        return remote(
            own.at[:, pl.ds(0, 2 * A)],
            tile.at[load],
            own_send.at[step],
            own_recv.at[step],
            (peer(step), gx, gy),
        )

    each_peer(lambda step: own_copy(step).start())

    row_copies = [
        (-1, remote(prior_in.at[0, :, pl.ds(0, 3)], rows_high, rows_send.at[0], rows_recv.at[0], toward(-1, 0))),
        (-1, remote(support_in.at[pl.ds(0, 2)], fixed_high, rows_send.at[1], rows_recv.at[1], toward(-1, 0))),
        (1, remote(prior_in.at[0, :, pl.ds(R - 2, 2)], rows_low, rows_send.at[2], rows_recv.at[2], toward(1, 0))),
        (1, remote(support_in.at[pl.ds(R - 1, 1)], fixed_low, rows_send.at[3], rows_recv.at[3], toward(1, 0))),
    ]
    column_copies = [
        (-1, remote(send_low, columns_high, column_send.at[0], column_recv.at[0], toward(0, -1))),
        (1, remote(send_high, columns_low, column_send.at[1], column_recv.at[1], toward(0, 1))),
    ]
    for dy, copy in column_copies:
        pl.when(inside(0, dy))(copy.start)
    for dx, copy in row_copies:
        pl.when(inside(dx, 0))(copy.start)

    def in_grid(row, columns):
        row, columns = row + gx * R, columns + gy * W
        return (row >= 0) & (row < n_x * R) & (columns >= 0) & (columns < n_y * W)

    def set_mask(row, carry):
        columns = lax.broadcasted_iota(jnp.int32, (48, A), 0) - 8
        mask[row] = jnp.where(in_grid(row - 8, columns), 1.0, 0.0)
        return carry

    lax.fori_loop(3, 21, set_mask, 0)

    def set_ring_mask(row, carry):
        lane = lanes((wide, A))
        layer = lax.broadcasted_iota(jnp.int32, (wide, A), 0) - 4 + load * depth
        kept = in_grid(row - 4, lane - 4) & (layer >= 0) & (layer < A) & (lane < W + 8)
        ring_mask[row] = jnp.where(kept, 1.0, 0.0)
        return carry

    lax.fori_loop(1, 15, set_ring_mask, 0)

    fetches[3].wait()
    fetches[4].wait()
    flat = load_nodes[...]
    column_bits = (n_y * W).bit_length() - 1
    node_row = lax.shift_right_logical(flat, 7 + column_bits) - gx * R + 1
    node_column = (lax.shift_right_logical(flat, 7) & (n_y * W - 1)) - gy * W + 2
    held = (node_row >= 0) & (node_row < 11) & (node_column >= 0) & (node_column < USED)
    spread[0:1, :] = jnp.where(held, node_row * USED + node_column, -1)
    spread[1:2, :] = flat & (A - 1)
    force[...] = jnp.zeros(force.shape, jnp.float32)

    def add_loads(index, carry):
        span = pl.ds(pl.multiple_of(index * CHUNK, CHUNK), CHUNK)
        place = spread[0:1, span]
        depth_of = spread[1:2, span]
        left = jnp.where(
            lax.broadcasted_iota(jnp.int32, (11 * USED, CHUNK), 0) == place, 1.0, 0.0
        ).astype(jnp.bfloat16)
        here = lax.broadcasted_iota(jnp.int32, (A, CHUNK), 0) == depth_of
        rest = [load_forces[c, :, span] for c in range(3)]
        for part in range(3):
            rights = []
            for c in range(3):
                rounded = rest[c].astype(jnp.bfloat16).astype(jnp.float32)
                rest[c] = rest[c] - rounded
                rights.append(jnp.where(here, rounded, 0.0).astype(jnp.bfloat16))
            force[...] += lax.dot_general(
                left,
                jnp.concatenate(rights, axis=0),
                (((1,), (1,)), ((), ())),
                preferred_element_type=jnp.float32,
            )
        return carry

    lax.fori_loop(0, load_nodes.shape[1] // CHUNK, add_loads, 0)

    for index, (dx, dy) in enumerate(AROUND):

        @pl.when(inside(dx, dy))
        def _():
            first_around[opposite[index]].wait_recv()

    lane = lanes((depth, A))
    halo[:, 0:A] = beside[0, :, A : 2 * A]
    halo[:, A : 2 * A] = beside[1, :, 0:A]
    halo[:, 2 * A : 3 * A] = jnp.where(lane < 64, beside[1, :, A : 2 * A], beside[0, :, 0:A])
    for index in range(3):
        at = (3 + index) * A
        halo[:, at : at + A] = jnp.where(lane < 64, packs[index, 1], packs[index, 0])
    halos[load] = halo[...]

    def halo_copy(step):
        return remote(
            halo, halos.at[load], halo_send.at[step], halo_recv.at[step], (peer(step), gx, gy)
        )

    each_peer(lambda step: halo_copy(step).start())

    for dy, copy in column_copies:
        other = column_copies[0][1] if dy == 1 else column_copies[1][1]
        pl.when(inside(0, dy))(other.wait_recv)
    corner_copies = []
    for dx in (-1, 1):
        for part, (source, target) in enumerate(
            ((columns_low, corners_low), (columns_high, corners_high))
        ):
            at = (dx + 1) + part
            corner_copies.append(
                (
                    dx,
                    remote(
                        source,
                        target.at[(1 - dx) // 2],
                        corner_send.at[at],
                        corner_recv.at[at],
                        toward(dx, 0),
                    ),
                )
            )
    for dx, copy in corner_copies:
        pl.when(inside(dx, 0))(copy.start)

    for ref in (wave, wave2, ring_wave, ring_wave2):

        def clear(row, carry):
            ref[row] = jnp.zeros(ref.shape[1:], jnp.float32)
            return carry

        lax.fori_loop(0, ref.shape[0], clear, 0)

    def clear_rows(row, carry):
        for c in range(3):
            field[c, row, W:PITCH, :] = jnp.zeros((PITCH - W, A), jnp.float32)
        free[row] = jnp.zeros((PITCH, A), jnp.float32)
        return carry

    lax.fori_loop(0, ROWS, clear_rows, 0)

    for c in range(3):
        for row in range(R):
            field[c, row + 2, 2 : 2 + W, :] = prior[0, c, row]
    for row in range(R):
        free[row + 2, 2 : 2 + W, :] = support[row].astype(jnp.float32)

    for dx, copy in row_copies + corner_copies:
        opposite_copy = {
            id(a[1]): b[1]
            for pairs in (
                (row_copies[0], row_copies[2]),
                (row_copies[1], row_copies[3]),
                (corner_copies[0], corner_copies[2]),
                (corner_copies[1], corner_copies[3]),
            )
            for a, b in (pairs, pairs[::-1])
        }[id(copy)]
        pl.when(inside(dx, 0))(opposite_copy.wait_recv)

    for c in range(3):
        for row in range(2):
            field[c, row, 2 : 2 + W, :] = rows_low[c, row]
        for row in range(3):
            field[c, row + 10, 2 : 2 + W, :] = rows_high[c, row]
    free[1, 2 : 2 + W, :] = fixed_low[0].astype(jnp.float32)
    for row in range(2):
        free[row + 10, 2 : 2 + W, :] = fixed_high[row].astype(jnp.float32)
    for row in range(-2, R + 3):
        if row < 0:
            low, high, at = corners_low.at[0], corners_high.at[0], row + R
        elif row < R:
            low, high, at = columns_low, columns_high, row
        else:
            low, high, at = corners_low.at[1], corners_high.at[1], row - R
        for c in range(3):
            field[c, row + 2, 0:2, :] = low[7 * at + 2 * c : 7 * at + 2 * c + 2, :]
            field[c, row + 2, 2 + W : 5 + W, :] = high[11 * at + 3 * c : 11 * at + 3 * c + 3, :]
        free[row + 2, 1:2, :] = low[7 * at + 6 : 7 * at + 7, :]
        free[row + 2, 2 + W : 4 + W, :] = high[11 * at + 9 : 11 * at + 11, :]

    def set_free(row, carry):
        columns = lax.broadcasted_iota(jnp.int32, (PITCH, A), 0) - 2
        kept = in_grid(row - 2, columns) & (columns >= -1) & (columns <= W + 1)
        free[row] = jnp.where(kept & (free[row] == 0.0), 1.0, 0.0)
        return carry

    lax.fori_loop(1, 12, set_free, 0)

    def lift(row, carry):
        for c in range(3):
            lifted[c, row] = lane_up(field[c, row])
        return carry

    lax.fori_loop(0, ROWS, lift, 0)

    def place(block, pieces):
        value = block.T
        for start, rows, columns, row, column in pieces:
            part = value[start : start + rows * columns].reshape(rows, columns, A)
            wave[row + 8 : row + 8 + rows, column + 16 : column + 16 + columns, :] = part

    each_peer(lambda step: own_copy(step).wait_recv())
    for half in range(2):
        place(tile[:, :, A * half : A * half + A].reshape(A, A), [(0, 4, W, 4 * half, 0)])
    each_peer(lambda step: halo_copy(step).wait_recv())
    layout = [
        [(0, 4, W, -4, 0)],
        [(0, 4, W, 8, 0)],
        [(0, 2, W, 12, 0), (64, 2, W, -6, 0)],
    ] + [[(0, 8, 8, dx * R, W), (64, 8, 8, dx * R, -8)] for dx in (-1, 0, 1)]
    for index, pieces in enumerate(layout):
        place(halos[:, :, A * index : A * index + A].reshape(A, A), pieces)

    theta, factors = chebyshev_factors()

    def start_filter(row, carry):
        source = wave[row, 8:56, :]
        direction = source / theta
        remain[row] = source
        result[row] = direction
        wave[row, 8:56, :] = direction
        return carry

    lax.fori_loop(2, 22, start_filter, 0)
    source, target = wave, wave2
    for sweep, (keep, gain) in enumerate(factors):

        def one_row(row, carry, source=source, target=target, keep=keep, gain=gain):
            middle = source[row, 8:56, :]
            near = (
                source[row - 1, 8:56, :]
                + source[row + 1, 8:56, :]
                + source[row, 7:55, :]
                + source[row, 9:57, :]
                + lane_up(middle)
                + lane_down(middle)
            )
            left = remain[row] - ((1.0 + 6.0 * filter_weight) * middle - filter_weight * near)
            direction = (keep * middle + gain * left) * mask[row]
            remain[row] = left
            result[row] = result[row] + direction
            target[row, 8:56, :] = direction
            return carry

        in_groups(3 + sweep, 21 - sweep, 3, one_row)
        source, target = target, source

    def set_modulus(row, carry):
        filtered = result[row + 6, 6 : 6 + USED, :]
        columns = lax.broadcasted_iota(jnp.int32, (USED, A), 0) - 2
        modulus[row, 0:8, :] = jnp.zeros((8, A), jnp.float32)
        modulus[row, 8 : 8 + USED, :] = jnp.where(
            in_grid(row - 2, columns), modulus_floor + filtered * filtered, 0.0
        )
        return carry

    lax.fori_loop(0, 12, set_modulus, 0)
    for half in range(2):
        tall = result[8 + 4 * half : 12 + 4 * half, 8 : 8 + W, :].reshape(A, A)
        weights[4 : 4 + A, A * half : A * half + A] = tall.T
    weights[0:4, :] = jnp.zeros((4, 2 * A), jnp.float32)
    weights[4 + A : 8 + A, :] = jnp.zeros((4, 2 * A), jnp.float32)

    def set_step(row, carry):
        around_node = total(
            [modulus[row - 1 + p, 7 + q : 7 + q + USED, :] for p in range(2) for q in range(2)]
        )
        around_node = around_node + lane_down(around_node)
        step_size[row] = relax_factor / ((lame + 4 * shear) / 9 * around_node)
        return carry

    lax.fori_loop(1, 12, set_step, 0)

    for sweep in range(JACOBI):
        first, last = 1 + sweep, 12 - sweep
        for block in range(BLOCKS):

            def one_element_row(row, carry, column=8 * block):
                low, pending = carry
                low = dict(zip(KEYS, low))
                high = plane_sums(field, lifted, row + 1, column)
                forces = element_forces(
                    row_coefs(low, high), modulus[row, pl.ds(column + 8, 8), :]
                )
                node = {}
                following = []
                for at, (c, q, r) in enumerate(KEYS):
                    change = forces[c, 1, q, r]
                    if (c, 0, q, r) in forces:
                        same = forces[c, 0, q, r]
                        node[c, q, r] = pending[at] + (same - change)
                        following.append(same + change)
                    else:
                        node[c, q, r] = pending[at] - change
                        following.append(change)
                for c in range(3):
                    for sign, near_to, far_to in (
                        (-1, near_part, far_part),
                        (1, near_upper, far_upper),
                    ):
                        sums, changes = (
                            node[c, q, 0] + node[c, q, 1] if sign > 0 else node[c, q, 0] - node[c, q, 1]
                            for q in range(2)
                        )
                        near_to[c, row, pl.ds(column, 8), :] = sums - changes
                        far_to[c, row, pl.ds(column + 1, 8), :] = sums + changes
                return [high[key] for key in KEYS], following

            low = plane_sums(field, lifted, first - 1, 8 * block)
            nothing = [jnp.zeros((8, A), jnp.float32)] * len(KEYS)
            in_groups(
                first - 1,
                last,
                (last - first + 1) // 2,
                one_element_row,
                ([low[key] for key in KEYS], nothing),
            )

        def one_node_row(row, carry):
            span = pl.ds(0, USED)
            rate = step_size[row]
            open_here = free[row, span, :] > 0.0
            for c in range(3):
                applied = near_part[c, row, span, :] + far_part[c, row, span, :]
                applied = applied + lane_down(near_upper[c, row, span, :] + far_upper[c, row, span, :])
                load_here = force[pl.ds(pl.multiple_of((row - 1) * USED, 8), USED), A * c : A * c + A]
                moved = field[c, row, span, :] + (load_here - applied) * rate
                moved = jnp.where(open_here, moved, 0.0)
                field[c, row, span, :] = moved
                lifted[c, row, span, :] = lane_up(moved)
            return carry

        in_groups(first, last, 2, one_node_row)

    for block in range(W // 8):

        def one_energy_row(row, low, column=8 * block + 2):
            high = plane_sums(field, lifted, row + 1, column)
            value = element_energy(row_coefs(dict(zip(KEYS, low)), high))
            remain[row, pl.ds(column - 2, 8), :] = value
            return [high[key] for key in KEYS]

        low = plane_sums(field, lifted, 2, 8 * block + 2)
        in_groups(2, 10, 4, one_energy_row, [low[key] for key in KEYS])
    for half in range(2):
        tall = remain[2 + 4 * half : 6 + 4 * half, 0:W, :].reshape(A, A)
        energy[4 : 4 + A, A * half : A * half + A] = tall.T
    energy[0:4, :] = jnp.zeros((4, 2 * A), jnp.float32)
    energy[4 + A : 8 + A, :] = jnp.zeros((4, 2 * A), jnp.float32)

    for c in range(3):
        for row in range(R):
            displacement[0, c, row] = field[c, row + 2, 2 : 2 + W, :]

    def slab(owner):
        return pl.ds(pl.multiple_of(owner * depth, 8), wide)

    def share_copy(step):
        return remote(
            energy.at[slab(peer(step)), :],
            shares.at[load],
            share_send.at[step],
            share_recv.at[step],
            (peer(step), gx, gy),
        )

    each_peer(lambda step: share_copy(step).start())
    shares[load] = energy[slab(load), :]
    each_peer(lambda step: share_copy(step).wait_recv())
    summed = total([shares[index] for index in range(n_load)])
    value = -(2.0 / n_load) * weights[slab(load), :] * summed
    share[...] = value
    share_pack[...] = edge_pack([value[:, 0:A], value[:, A : 2 * A]])

    last_around = [
        around(index, beside2, packs2, last_send, last_recv, share, share_pack)
        for index in range(8)
    ]
    for index, (dx, dy) in enumerate(AROUND):

        @pl.when(inside(dx, dy))
        def _():
            last_around[index].start()

    for index, (dx, dy) in enumerate(AROUND):

        @pl.when(inside(dx, dy))
        def _():
            last_around[opposite[index]].wait_recv()

    lane = lanes((wide, A))
    for row in range(-4, R + 4):
        if row < 0:
            body, pack = beside2[0, :, A : 2 * A], 0
        elif row < R:
            body, pack = share[:, A * (row // 4) : A * (row // 4) + A], 1
        else:
            body, pack = beside2[1, :, 0:A], 2
        at = row % R
        line = turned(body, 4 - W * (at % 4))
        after = turned(packs2[pack, 1], 4 + W - 8 * at)
        before = turned(packs2[pack, 0], -4 - 64 - 8 * at)
        line = jnp.where(lane < 4, before, line)
        line = jnp.where(lane >= W + 4, after, line)
        line = jnp.where(lane < W + 8, line, 0.0)
        direction = line / theta
        ring_remain[row + 4] = line
        ring_result[row + 4] = direction
        ring_wave[row + 4, 8 : 8 + wide, :] = direction

    source, target = ring_wave, ring_wave2
    for sweep, (keep, gain) in enumerate(factors):

        def one_ring_row(row, carry, source=source, target=target, keep=keep, gain=gain):
            middle = source[row, 8 : 8 + wide, :]
            near = (
                source[row - 1, 8 : 8 + wide, :]
                + source[row + 1, 8 : 8 + wide, :]
                + source[row, 7 : 7 + wide, :]
                + source[row, 9 : 9 + wide, :]
                + pltpu.roll(middle, A - 1, 1)
                + pltpu.roll(middle, 1, 1)
            )
            left = ring_remain[row] - (
                (1.0 + 6.0 * filter_weight) * middle - filter_weight * near
            )
            direction = (keep * middle + gain * left) * ring_mask[row]
            ring_remain[row] = left
            ring_result[row] = ring_result[row] + direction
            target[row, 8 : 8 + wide, :] = direction
            return carry

        in_groups(1 + sweep, 15 - sweep, 14, one_ring_row)
        source, target = target, source
    for row in range(R):
        moved = turned(ring_result[row + 4], -4)
        raw[row] = moved[4 : 4 + depth]
        sensitivity[row] = raw[row, :, 0:W]

    for index, (dx, dy) in enumerate(AROUND):

        @pl.when(inside(dx, dy))
        def _():
            first_around[index].wait_send()
            last_around[index].wait_send()

    for dx, copy in row_copies + corner_copies:
        pl.when(inside(dx, 0))(copy.wait_send)
    for dy, copy in column_copies:
        pl.when(inside(0, dy))(copy.wait_send)
    each_peer(lambda step: own_copy(step).wait_send())
    each_peer(lambda step: halo_copy(step).wait_send())
    each_peer(lambda step: share_copy(step).wait_send())


def body(counts, density, displacement_prior, support, load_nodes, load_forces):
    n_load = counts[0]
    depth = A // n_load
    wide = depth + 8
    picks = load_nodes.shape[1]
    real, whole = jnp.float32, jnp.int32
    scratch = [
        ((R, depth, W), real),
        (displacement_prior.shape, real),
        ((R, W, A), whole),
        ((1, picks), whole),
        ((3, 1, picks), real),
        ((R, depth, A), real),
        ((depth, 3 * A), real),
        ((n_load, depth, 2 * A), real),
        ((2, depth, 2 * A), real),
        ((3, 2, depth, A), real),
        ((depth, 6 * A), real),
        ((n_load, depth, 6 * A), real),
        ((24, 64, A), real),
        ((24, 64, A), real),
        ((24, 48, A), real),
        ((24, 48, A), real),
        ((3, 2, W, A), real),
        ((3, 3, W, A), real),
        ((1, W, A), whole),
        ((2, W, A), whole),
        ((11 * R, A), real),
        ((7 * R, A), real),
        ((7 * R, A), real),
        ((11 * R, A), real),
        ((2, 7 * R, A), real),
        ((2, 11 * R, A), real),
        ((3, ROWS, PITCH, A), real),
        ((3, ROWS, PITCH, A), real),
        ((3, ROWS, PITCH, A), real),
        ((12, 8 + USED, A), real),
        ((ROWS, PITCH, A), real),
        ((12, USED, A), real),
        ((11 * USED, 3 * A), real),
        ((8, picks), whole),
        ((A + 8, 2 * A), real),
        ((n_load, wide, 2 * A), real),
        ((A + 8, 2 * A), real),
        ((wide, 2 * A), real),
        ((wide, A), real),
        ((2, wide, 2 * A), real),
        ((3, 2, wide, A), real),
        ((16, wide + 16, A), real),
        ((16, wide + 16, A), real),
        ((16, wide, A), real),
        ((16, wide, A), real),
        ((3, ROWS, PITCH, A), real),
        ((3, ROWS, PITCH, A), real),
        ((3, ROWS, PITCH, A), real),
        ((24, 48, A), real),
        ((16, wide, A), real),
    ]
    semaphores = [8, 8, n_load, n_load, n_load, n_load, 4, 4, 2, 2, 4, 4, n_load, n_load, 8, 8, 5]
    displacement, sensitivity = pl.pallas_call(
        functools.partial(kernel, counts, depth),
        out_shape=(
            jax.ShapeDtypeStruct(displacement_prior.shape, real),
            jax.ShapeDtypeStruct((R, depth, W), real),
        ),
        in_specs=[pl.BlockSpec(memory_space=pltpu.HBM)] * 5,
        out_specs=(pl.BlockSpec(memory_space=pltpu.VMEM),) * 2,
        scratch_shapes=[pltpu.VMEM(shape, kind) for shape, kind in scratch]
        + [pltpu.SemaphoreType.DMA((count,)) for count in semaphores],
        compiler_params=pltpu.CompilerParams(
            collective_id=0, has_side_effects=True, vmem_limit_bytes=48 << 20
        ),
        name="elasticity",
    )(
        jnp.transpose(density, (0, 2, 1)),
        displacement_prior,
        support,
        load_nodes,
        jnp.transpose(load_forces, (1, 0, 2)),
    )
    return displacement, jnp.transpose(sensitivity, (0, 2, 1))


def solution(mesh):
    counts = tuple(mesh.shape[axis] for axis in ("load", "gx", "gy"))
    return jax.shard_map(
        functools.partial(body, counts),
        mesh=mesh,
        in_specs=(
            P("gx", "gy", "load"),
            P("load", None, "gx", "gy", None),
            P("gx", "gy", None),
            P("load", None),
            P("load", None, None),
        ),
        out_specs=(P("load", None, "gx", "gy", None), P("gx", "gy", "load")),
        check_vma=False,
    )
```

```python
import functools

import jax
import jax.numpy as jnp
from jax import lax
from jax.experimental import pallas as pl
from jax.experimental.pallas import tpu as pltpu
from jax.sharding import PartitionSpec as P

SWEEPS = 4
JACOBI = 2

poisson_ratio = 0.3
filter_weight = 3.0
relax_factor = 0.6
modulus_floor = 0.05
lame = poisson_ratio / ((1 + poisson_ratio) * (1 - 2 * poisson_ratio))
shear = 1.0 / (2 * (1 + poisson_ratio))

R = 8
W = 32
A = 128
N = 3 * R * W
ROWS = 13
PITCH = 48
USED = 40
BLOCKS = USED // 8
CHUNK = 512
MESH = pl.DeviceIdType.MESH
AROUND = [(0, -1), (0, 1), (-1, -1), (-1, 1), (1, -1), (1, 1), (-1, 0), (1, 0)]


def chebyshev_factors():
    theta = 1.0 + 6.0 * filter_weight
    delta = 6.0 * filter_weight
    sigma = theta / delta
    ratio = 1.0 / sigma
    steps = []
    for _ in range(SWEEPS):
        following = 1.0 / (2.0 * sigma - ratio)
        steps.append((following * ratio, 2.0 * following / delta))
        ratio = following
    return theta, steps


def chebyshev_terms():
    theta, steps = chebyshev_factors()
    terms = []
    before = None
    for keep, gain in steps:
        own, last = keep - gain * theta, 0.0
        if before is None:
            own += gain * theta
        else:
            own += gain / before[1]
            last = -gain / before[1] * before[0]
        terms.append((own, last, gain * filter_weight))
        before = keep, gain
    return theta, terms


def lanes(shape):
    return lax.broadcasted_iota(jnp.int32, shape, len(shape) - 1)


def lane_up(x):
    return jnp.where(lanes(x.shape) == A - 1, 0.0, pltpu.roll(x, A - 1, x.ndim - 1))


def lane_down(x):
    return jnp.where(lanes(x.shape) == 0, 0.0, pltpu.roll(x, 1, x.ndim - 1))


def fold_pack(halves):
    wide = halves[0].shape[0]
    lane = lanes((wide, A))
    packed = jnp.zeros((wide, A), jnp.float32)
    for row in range(R):
        at = W * (row % 4)
        for start, column in ((4 * row, 0), (64 + 4 * row, W - 4)):
            moved = turned(halves[row // 4], start - at - column)
            packed = jnp.where((lane >= start) & (lane < start + 4), moved, packed)
    if wide != 16:
        return packed
    lane = lanes((8, A))
    return jnp.where((lane & 32) == 0, packed[0:8], turned(packed[8:16], 32))


def unfolded(pack, steps):
    if pack.shape[0] != 8:
        return turned(pack, steps)
    return jnp.concatenate([turned(pack, steps), turned(pack, steps - 32)], axis=0)


def turned(x, steps):
    steps %= A
    return pltpu.roll(x, steps, 1) if steps else x


def edge_pack(halves):
    lane = lanes(halves[0].shape)
    packed = jnp.zeros(halves[0].shape, jnp.float32)
    for row in range(R):
        at = W * (row % 4)
        for start, column in ((8 * row, 0), (64 + 8 * row, W - 8)):
            moved = turned(halves[row // 4], start - at - column)
            packed = jnp.where((lane >= start) & (lane < start + 8), moved, packed)
    return packed


def peers_of(count):
    side = 4 if count == 16 else count
    steps = [(a, b) for a in range(count // side) for b in range(side)][1:]

    def hops(step):
        return min(step[0], count // side - step[0]) + min(step[1], side - step[1])

    return side, sorted(steps, key=hops, reverse=True)


def total(values):
    result = values[0]
    for value in values[1:]:
        result = result + value
    return result


def groups():
    return [
        ([(0, 1, 0, 0), (1, 0, 1, 0), (2, 0, 0, 1)], lame / 16, 2 * shear / 16),
        ([(0, 0, 1, 0), (1, 1, 0, 0)], shear / 16, None),
        ([(0, 0, 0, 1), (2, 1, 0, 0)], shear / 16, None),
        ([(1, 0, 0, 1), (2, 0, 1, 0)], shear / 16, None),
        ([(0, 0, 1, 1), (1, 1, 0, 1), (2, 1, 1, 0)], shear / 48, shear / 48),
        ([(0, 1, 0, 1), (1, 0, 1, 1)], lame / 48, 3 * shear / 48),
        ([(0, 1, 1, 0), (2, 0, 1, 1)], lame / 48, 3 * shear / 48),
        ([(1, 1, 1, 0), (2, 1, 0, 1)], lame / 48, 3 * shear / 48),
        ([(0, 1, 1, 1)], None, (lame + 4 * shear) / 144),
        ([(1, 1, 1, 1)], None, (lame + 4 * shear) / 144),
        ([(2, 1, 1, 1)], None, (lame + 4 * shear) / 144),
    ]


def element_forces(coefs, modulus):
    scaled = {}

    def times(weight, value):
        if weight not in scaled:
            scaled[weight] = modulus * weight
        return scaled[weight] * value

    forces = {}
    for members, joint, single in groups():
        if joint is not None:
            common = total([coefs[m] for m in members])
            if joint == single:
                for m in members:
                    forces[m] = times(joint, common + coefs[m])
                continue
            common = times(joint, common)
            for m in members:
                forces[m] = common if single is None else common + times(single, coefs[m])
        else:
            for m in members:
                forces[m] = times(single, coefs[m])
    return forces


def element_energy(coefs):
    terms = {}
    for members, joint, single in groups():
        if joint is not None:
            common = total([coefs[m] for m in members])
            terms.setdefault(joint, []).append(common * common)
        if single is not None:
            for m in members:
                terms.setdefault(single, []).append(coefs[m] * coefs[m])
    return total([weight * total(values) for weight, values in terms.items()])


def plane_sums(field, lifted, row, column):
    out = {}
    for c in range(3):
        near = field[c, row, pl.ds(column, 8), :]
        far = field[c, row, pl.ds(column + 1, 8), :]
        near_up = lifted[c, row, pl.ds(column, 8), :]
        far_up = lifted[c, row, pl.ds(column + 1, 8), :]
        for q, value, up in ((0, near + far, near_up + far_up), (1, far - near, far_up - near_up)):
            out[c, q, 0] = value + up
            out[c, q, 1] = up - value
    return out


def in_groups(first, last, size, action, carry=0):
    trips = (last - first) // size

    def trip(index, carry):
        for at in range(size):
            carry = action(first + index * size + at, carry)
        return carry

    if trips > 1:
        carry = lax.fori_loop(0, trips, trip, carry)
        first += trips * size
    for row in range(first, last):
        carry = action(row, carry)
    return carry


KEYS = [(c, q, r) for c in range(3) for q in range(2) for r in range(2)]


def row_coefs(low, high):
    coefs = {}
    for c, q, r in KEYS:
        coefs[c, 0, q, r] = low[c, q, r] + high[c, q, r]
        coefs[c, 1, q, r] = high[c, q, r] - low[c, q, r]
    return coefs


def kernel(
    counts,
    depth,
    density_in,
    prior_in,
    support_in,
    nodes_in,
    forces_in,
    displacement,
    sensitivity,
    density,
    prior,
    support,
    load_nodes,
    load_forces,
    raw,
    own,
    tile,
    beside,
    packs,
    halo,
    halos,
    wave0,
    wave1,
    wave2,
    wave3,
    wave4,
    remain,
    result,
    rows_low,
    rows_high,
    fixed_low,
    fixed_high,
    send_low,
    send_high,
    columns_low,
    columns_high,
    corners_low,
    corners_high,
    field,
    near_part,
    far_part,
    modulus,
    free,
    step_size,
    force,
    spread,
    energy,
    shares,
    weights,
    share,
    share_pack,
    beside2,
    packs2,
    ring_wave0,
    ring_wave1,
    ring_wave2,
    ring_wave3,
    ring_wave4,
    lifted,
    near_upper,
    far_upper,
    mask,
    ring_mask,
    around_send,
    around_recv,
    own_send,
    own_recv,
    halo_send,
    halo_recv,
    rows_send,
    rows_recv,
    column_send,
    column_recv,
    corner_send,
    corner_recv,
    share_send,
    share_recv,
    last_send,
    last_recv,
    fetched,
):
    n_load, n_x, n_y = counts
    waves = [wave0, wave1, wave2, wave3, wave4]
    wave = wave0
    ring_waves = [ring_wave0, ring_wave1, ring_wave2, ring_wave3, ring_wave4]
    wide = depth + 8
    load, gx, gy = lax.axis_index("load"), lax.axis_index("gx"), lax.axis_index("gy")

    def inside(dx, dy):
        return (gx + dx >= 0) & (gx + dx < n_x) & (gy + dy >= 0) & (gy + dy < n_y)

    side, steps = peers_of(n_load)

    def peer(step):
        a, b = steps[step]
        across = lax.rem(lax.div(load, side) + a, n_load // side)
        return across * side + lax.rem(lax.rem(load, side) + b, side)

    def each_peer(action):
        for step in range(n_load - 1):
            action(step)

    def remote(src, dst, send, recv, where):
        return pltpu.make_async_remote_copy(
            src_ref=src,
            dst_ref=dst,
            send_sem=send,
            recv_sem=recv,
            device_id=where,
            device_id_type=MESH,
        )

    def toward(dx, dy):
        return (load, gx + dx, gy + dy)

    fetches = [
        pltpu.make_async_copy(source, target, fetched.at[index])
        for index, (source, target) in enumerate(
            (
                (density_in, density),
                (prior_in, prior),
                (support_in, support),
                (nodes_in, load_nodes),
                (forces_in, load_forces),
            )
        )
    ]
    for fetch in fetches:
        fetch.start()

    for index, (dx, dy) in enumerate(AROUND):

        @pl.when(jnp.logical_not(inside(dx, dy)))
        def _():
            if dy == 0:
                for ref in (beside, beside2):
                    ref[(dx + 1) // 2] = jnp.zeros(ref.shape[1:], jnp.float32)
            else:
                for ref in (packs, packs2):
                    ref[dx + 1, (dy + 1) // 2] = jnp.zeros(ref.shape[2:], jnp.float32)

    @pl.when(jnp.logical_not(inside(-1, 0)))
    def _():
        rows_low[...] = jnp.zeros(rows_low.shape, jnp.float32)
        fixed_low[...] = jnp.zeros(fixed_low.shape, jnp.int32)
        corners_low[0] = jnp.zeros(corners_low.shape[1:], jnp.float32)
        corners_high[0] = jnp.zeros(corners_high.shape[1:], jnp.float32)

    @pl.when(jnp.logical_not(inside(1, 0)))
    def _():
        rows_high[...] = jnp.zeros(rows_high.shape, jnp.float32)
        fixed_high[...] = jnp.zeros(fixed_high.shape, jnp.int32)
        corners_low[1] = jnp.zeros(corners_low.shape[1:], jnp.float32)
        corners_high[1] = jnp.zeros(corners_high.shape[1:], jnp.float32)

    @pl.when(jnp.logical_not(inside(0, -1)))
    def _():
        columns_low[...] = jnp.zeros(columns_low.shape, jnp.float32)

    @pl.when(jnp.logical_not(inside(0, 1)))
    def _():
        columns_high[...] = jnp.zeros(columns_high.shape, jnp.float32)

    barrier = pltpu.get_barrier_semaphore()
    each_peer(
        lambda step: pl.semaphore_signal(
            barrier, inc=1, device_id=(peer(step), gx, gy), device_id_type=MESH
        )
    )
    expected = n_load - 1
    for dx, dy in AROUND:
        expected = expected + inside(dx, dy).astype(jnp.int32)

        @pl.when(inside(dx, dy))
        def _():
            pl.semaphore_signal(
                barrier, inc=1, device_id=toward(dx, dy), device_id_type=MESH
            )

    fetches[0].wait()
    for row in range(R):
        raw[row, :, 0:W] = density[row]
    halves = []
    for half in range(2):
        value = jnp.zeros((depth, A), jnp.float32)
        lane = lanes(value.shape)
        for row in range(4):
            moved = turned(raw[4 * half + row], W * row)
            value = jnp.where((lane >= W * row) & (lane < W * row + W), moved, value)
        halves.append(value)
        own[:, A * half : A * half + A] = value
        tile[load, :, A * half : A * half + A] = value
    own[:, 2 * A : 3 * A] = edge_pack(halves)

    fetches[1].wait()
    fetches[2].wait()

    for row in range(R):
        for c in range(3):
            send_low[11 * row + 3 * c : 11 * row + 3 * c + 3, :] = prior[0, c, row, 0:3, :]
            send_high[7 * row + 2 * c : 7 * row + 2 * c + 2, :] = prior[0, c, row, W - 2 : W, :]
        send_low[11 * row + 9 : 11 * row + 11, :] = support[row, 0:2, :].astype(jnp.float32)
        send_high[7 * row + 6 : 7 * row + 7, :] = support[row, W - 1 : W, :].astype(jnp.float32)

    pl.semaphore_wait(barrier, expected)

    def around(index, whole, narrow, send, recv, sources, pack):
        dx, dy = AROUND[index]
        if dy == 0:
            return remote(
                sources[(1 + dx) // 2], whole.at[(1 - dx) // 2], send.at[index], recv.at[index], toward(dx, dy)
            )
        return remote(
            pack, narrow.at[1 - dx, (1 - dy) // 2], send.at[index], recv.at[index], toward(dx, dy)
        )

    first_around = [
        around(
            index,
            beside,
            packs,
            around_send,
            around_recv,
            [own.at[:, pl.ds(0, 2 * A)]] * 2,
            own.at[:, pl.ds(2 * A, A)],
        )
        for index in range(8)
    ]
    opposite = [AROUND.index((-dx, -dy)) for dx, dy in AROUND]

    for index, (dx, dy) in enumerate(AROUND):

        @pl.when(inside(dx, dy))
        def _():
            first_around[index].start()

    def own_copy(step):
        return remote(
            own.at[:, pl.ds(0, 2 * A)],
            tile.at[load],
            own_send.at[step],
            own_recv.at[step],
            (peer(step), gx, gy),
        )

    each_peer(lambda step: own_copy(step).start())

    row_copies = [
        (-1, remote(prior_in.at[0, :, pl.ds(0, 3)], rows_high, rows_send.at[0], rows_recv.at[0], toward(-1, 0))),
        (-1, remote(support_in.at[pl.ds(0, 2)], fixed_high, rows_send.at[1], rows_recv.at[1], toward(-1, 0))),
        (1, remote(prior_in.at[0, :, pl.ds(R - 2, 2)], rows_low, rows_send.at[2], rows_recv.at[2], toward(1, 0))),
        (1, remote(support_in.at[pl.ds(R - 1, 1)], fixed_low, rows_send.at[3], rows_recv.at[3], toward(1, 0))),
    ]
    column_copies = [
        (-1, remote(send_low, columns_high, column_send.at[0], column_recv.at[0], toward(0, -1))),
        (1, remote(send_high, columns_low, column_send.at[1], column_recv.at[1], toward(0, 1))),
    ]
    for dy, copy in column_copies:
        pl.when(inside(0, dy))(copy.start)
    for dx, copy in row_copies:
        pl.when(inside(dx, 0))(copy.start)

    def in_grid(row, columns):
        row, columns = row + gx * R, columns + gy * W
        return (row >= 0) & (row < n_x * R) & (columns >= 0) & (columns < n_y * W)

    def set_mask(row, carry):
        columns = lax.broadcasted_iota(jnp.int32, (48, A), 0) - 8
        mask[row] = jnp.where(in_grid(row - 8, columns), 1.0, 0.0)
        return carry

    lax.fori_loop(3, 21, set_mask, 0)

    def set_ring_mask(row, carry):
        lane = lanes((wide, A))
        layer = lax.broadcasted_iota(jnp.int32, (wide, A), 0) - 4 + load * depth
        kept = in_grid(row - 4, lane - 4) & (layer >= 0) & (layer < A) & (lane < W + 8)
        ring_mask[row] = jnp.where(kept, 1.0, 0.0)
        return carry

    lax.fori_loop(1, 15, set_ring_mask, 0)

    def halo_copy(step, part):
        span = pl.ds(part * 3 * A, 3 * A)
        return remote(
            halo.at[:, span],
            halos.at[load, :, span],
            halo_send.at[part, step],
            halo_recv.at[part, step],
            (peer(step), gx, gy),
        )

    for index, (dx, dy) in enumerate(AROUND):
        if dy == 0:

            @pl.when(inside(dx, dy))
            def _():
                first_around[opposite[index]].wait_recv()

    lane = lanes((depth, A))
    halo[:, 0:A] = beside[0, :, A : 2 * A]
    halo[:, A : 2 * A] = beside[1, :, 0:A]
    halo[:, 2 * A : 3 * A] = jnp.where(lane < 64, beside[1, :, A : 2 * A], beside[0, :, 0:A])
    halos[load, :, 0 : 3 * A] = halo[:, 0 : 3 * A]
    each_peer(lambda step: halo_copy(step, 0).start())

    fetches[3].wait()
    fetches[4].wait()
    flat = load_nodes[...]
    column_bits = (n_y * W).bit_length() - 1
    node_row = lax.shift_right_logical(flat, 7 + column_bits) - gx * R + 1
    node_column = (lax.shift_right_logical(flat, 7) & (n_y * W - 1)) - gy * W + 2
    held = (node_row >= 0) & (node_row < 11) & (node_column >= 0) & (node_column < USED)
    spread[0:1, :] = jnp.where(held, node_row * USED + node_column, -1)
    spread[1:2, :] = flat & (A - 1)
    force[...] = jnp.zeros(force.shape, jnp.float32)

    def add_loads(index, carry):
        span = pl.ds(pl.multiple_of(index * CHUNK, CHUNK), CHUNK)
        place = spread[0:1, span]
        depth_of = spread[1:2, span]
        left = jnp.where(
            lax.broadcasted_iota(jnp.int32, (11 * USED, CHUNK), 0) == place, 1.0, 0.0
        ).astype(jnp.bfloat16)
        here = lax.broadcasted_iota(jnp.int32, (A, CHUNK), 0) == depth_of
        rest = [load_forces[c, :, span] for c in range(3)]
        for part in range(3):
            rights = []
            for c in range(3):
                rounded = rest[c].astype(jnp.bfloat16).astype(jnp.float32)
                rest[c] = rest[c] - rounded
                rights.append(jnp.where(here, rounded, 0.0).astype(jnp.bfloat16))
            force[...] += lax.dot_general(
                left,
                jnp.concatenate(rights, axis=0),
                (((1,), (1,)), ((), ())),
                preferred_element_type=jnp.float32,
            )
        return carry

    lax.fori_loop(0, load_nodes.shape[1] // CHUNK, add_loads, 0)

    for index, (dx, dy) in enumerate(AROUND):
        if dy != 0:

            @pl.when(inside(dx, dy))
            def _():
                first_around[opposite[index]].wait_recv()

    for index in range(3):
        at = (3 + index) * A
        halo[:, at : at + A] = jnp.where(lane < 64, packs[index, 1], packs[index, 0])
        halos[load, :, at : at + A] = halo[:, at : at + A]
    each_peer(lambda step: halo_copy(step, 1).start())

    for dy, copy in column_copies:
        other = column_copies[0][1] if dy == 1 else column_copies[1][1]
        pl.when(inside(0, dy))(other.wait_recv)
    corner_copies = []
    for dx in (-1, 1):
        for part, (source, target) in enumerate(
            ((columns_low, corners_low), (columns_high, corners_high))
        ):
            at = (dx + 1) + part
            corner_copies.append(
                (
                    dx,
                    remote(
                        source,
                        target.at[(1 - dx) // 2],
                        corner_send.at[at],
                        corner_recv.at[at],
                        toward(dx, 0),
                    ),
                )
            )
    for dx, copy in corner_copies:
        pl.when(inside(dx, 0))(copy.start)

    for ref in waves[:4] + ring_waves[:4]:

        def clear(row, carry):
            ref[row] = jnp.zeros(ref.shape[1:], jnp.float32)
            return carry

        lax.fori_loop(0, ref.shape[0], clear, 0)

    def clear_rows(row, carry):
        for c in range(3):
            field[c, row, W:PITCH, :] = jnp.zeros((PITCH - W, A), jnp.float32)
        free[row] = jnp.zeros((PITCH, A), jnp.float32)
        return carry

    lax.fori_loop(0, ROWS, clear_rows, 0)

    for c in range(3):
        for row in range(R):
            field[c, row + 2, 2 : 2 + W, :] = prior[0, c, row]
    for row in range(R):
        free[row + 2, 2 : 2 + W, :] = support[row].astype(jnp.float32)

    for dx, copy in row_copies + corner_copies:
        opposite_copy = {
            id(a[1]): b[1]
            for pairs in (
                (row_copies[0], row_copies[2]),
                (row_copies[1], row_copies[3]),
                (corner_copies[0], corner_copies[2]),
                (corner_copies[1], corner_copies[3]),
            )
            for a, b in (pairs, pairs[::-1])
        }[id(copy)]
        pl.when(inside(dx, 0))(opposite_copy.wait_recv)

    for c in range(3):
        for row in range(2):
            field[c, row, 2 : 2 + W, :] = rows_low[c, row]
        for row in range(3):
            field[c, row + 10, 2 : 2 + W, :] = rows_high[c, row]
    free[1, 2 : 2 + W, :] = fixed_low[0].astype(jnp.float32)
    for row in range(2):
        free[row + 10, 2 : 2 + W, :] = fixed_high[row].astype(jnp.float32)
    for row in range(-2, R + 3):
        if row < 0:
            low, high, at = corners_low.at[0], corners_high.at[0], row + R
        elif row < R:
            low, high, at = columns_low, columns_high, row
        else:
            low, high, at = corners_low.at[1], corners_high.at[1], row - R
        for c in range(3):
            field[c, row + 2, 0:2, :] = low[7 * at + 2 * c : 7 * at + 2 * c + 2, :]
            field[c, row + 2, 2 + W : 5 + W, :] = high[11 * at + 3 * c : 11 * at + 3 * c + 3, :]
        free[row + 2, 1:2, :] = low[7 * at + 6 : 7 * at + 7, :]
        free[row + 2, 2 + W : 4 + W, :] = high[11 * at + 9 : 11 * at + 11, :]

    def set_free(row, carry):
        columns = lax.broadcasted_iota(jnp.int32, (PITCH, A), 0) - 2
        kept = in_grid(row - 2, columns) & (columns >= -1) & (columns <= W + 1)
        free[row] = jnp.where(kept & (free[row] == 0.0), 1.0, 0.0)
        return carry

    lax.fori_loop(1, 12, set_free, 0)

    def lift(row, carry):
        for c in range(3):
            lifted[c, row] = lane_up(field[c, row])
        return carry

    lax.fori_loop(0, ROWS, lift, 0)

    def place(block, pieces):
        value = block.T
        for start, rows, columns, row, column in pieces:
            part = value[start : start + rows * columns].reshape(rows, columns, A)
            wave[row + 8 : row + 8 + rows, column + 16 : column + 16 + columns, :] = part

    each_peer(lambda step: own_copy(step).wait_recv())
    for half in range(2):
        place(tile[:, :, A * half : A * half + A].reshape(A, A), [(0, 4, W, 4 * half, 0)])
    layout = [
        [(0, 4, W, -4, 0)],
        [(0, 4, W, 8, 0)],
        [(0, 2, W, 12, 0), (64, 2, W, -6, 0)],
    ] + [[(0, 8, 8, dx * R, W), (64, 8, 8, dx * R, -8)] for dx in (-1, 0, 1)]
    for index, pieces in enumerate(layout):
        if index % 3 == 0:
            each_peer(lambda step: halo_copy(step, index // 3).wait_recv())
        place(halos[:, :, A * index : A * index + A].reshape(A, A), pieces)

    theta, terms = chebyshev_terms()

    def start_filter(row, carry):
        wave[row, 8:56, :] = wave[row, 8:56, :] / theta
        return carry

    in_groups(2, 22, 5, start_filter)
    for sweep, (own_factor, last_factor, near_factor) in enumerate(terms):

        def one_row(row, carry, source=waves[sweep], target=waves[sweep + 1]):
            middle = source[row, 8:56, :]
            near = (
                source[row - 1, 8:56, :]
                + source[row + 1, 8:56, :]
                + source[row, 7:55, :]
                + source[row, 9:57, :]
                + lane_up(middle)
                + lane_down(middle)
            )
            direction = own_factor * middle + near_factor * near
            if sweep:
                direction = direction + last_factor * waves[sweep - 1][row, 8:56, :]
            target[row, 8:56, :] = direction * mask[row]
            return carry

        in_groups(3 + sweep, 21 - sweep, 3, one_row)

    def set_modulus(row, carry):
        filtered = total([ref[row + 6, 14 : 14 + USED, :] for ref in waves])
        result[row] = filtered
        columns = lax.broadcasted_iota(jnp.int32, (USED, A), 0) - 2
        modulus[row, 0:8, :] = jnp.zeros((8, A), jnp.float32)
        modulus[row, 8 : 8 + USED, :] = jnp.where(
            in_grid(row - 2, columns), modulus_floor + filtered * filtered, 0.0
        )
        return carry

    in_groups(0, 12, 3, set_modulus)
    for half in range(2):
        tall = result[2 + 4 * half : 6 + 4 * half, 2 : 2 + W, :].reshape(A, A)
        weights[4 : 4 + A, A * half : A * half + A] = tall.T
    weights[0:4, :] = jnp.zeros((4, 2 * A), jnp.float32)
    weights[4 + A : 8 + A, :] = jnp.zeros((4, 2 * A), jnp.float32)

    def set_step(row, carry):
        around_node = total(
            [modulus[row - 1 + p, 7 + q : 7 + q + USED, :] for p in range(2) for q in range(2)]
        )
        around_node = around_node + lane_down(around_node)
        step_size[row] = relax_factor / ((lame + 4 * shear) / 9 * around_node)
        return carry

    in_groups(1, 12, 4, set_step)

    for sweep in range(JACOBI):
        first, last = 1 + sweep, 12 - sweep
        for block in range(BLOCKS):

            def one_element_row(row, carry, column=8 * block):
                low, pending = carry
                low = dict(zip(KEYS, low))
                high = plane_sums(field, lifted, row + 1, column)
                forces = element_forces(
                    row_coefs(low, high), modulus[row, pl.ds(column + 8, 8), :]
                )
                node = {}
                following = []
                for at, (c, q, r) in enumerate(KEYS):
                    change = forces[c, 1, q, r]
                    if (c, 0, q, r) in forces:
                        same = forces[c, 0, q, r]
                        node[c, q, r] = pending[at] + (same - change)
                        following.append(same + change)
                    else:
                        node[c, q, r] = pending[at] - change
                        following.append(change)
                for c in range(3):
                    for sign, near_to, far_to in (
                        (-1, near_part, far_part),
                        (1, near_upper, far_upper),
                    ):
                        sums, changes = (
                            node[c, q, 0] + node[c, q, 1] if sign > 0 else node[c, q, 0] - node[c, q, 1]
                            for q in range(2)
                        )
                        near_to[c, row, pl.ds(column, 8), :] = sums - changes
                        far_to[c, row, pl.ds(column + 1, 8), :] = sums + changes
                return [high[key] for key in KEYS], following

            low = plane_sums(field, lifted, first - 1, 8 * block)
            nothing = [jnp.zeros((8, A), jnp.float32)] * len(KEYS)
            in_groups(
                first - 1,
                last,
                (last - first + 1) // 2,
                one_element_row,
                ([low[key] for key in KEYS], nothing),
            )

        def one_node_row(row, carry):
            span = pl.ds(0, USED)
            rate = step_size[row]
            open_here = free[row, span, :] > 0.0
            for c in range(3):
                applied = near_part[c, row, span, :] + far_part[c, row, span, :]
                applied = applied + lane_down(near_upper[c, row, span, :] + far_upper[c, row, span, :])
                load_here = force[pl.ds(pl.multiple_of((row - 1) * USED, 8), USED), A * c : A * c + A]
                moved = field[c, row, span, :] + (load_here - applied) * rate
                moved = jnp.where(open_here, moved, 0.0)
                field[c, row, span, :] = moved
                lifted[c, row, span, :] = lane_up(moved)
            return carry

        in_groups(first, last, 2, one_node_row)

    for block in range(W // 8):

        def one_energy_row(row, low, column=8 * block + 2):
            high = plane_sums(field, lifted, row + 1, column)
            value = element_energy(row_coefs(dict(zip(KEYS, low)), high))
            remain[row, pl.ds(column - 2, 8), :] = value
            return [high[key] for key in KEYS]

        low = plane_sums(field, lifted, 2, 8 * block + 2)
        in_groups(2, 10, 4, one_energy_row, [low[key] for key in KEYS])
    for half in range(2):
        tall = remain[2 + 4 * half : 6 + 4 * half, 0:W, :].reshape(A, A)
        energy[4 : 4 + A, A * half : A * half + A] = tall.T
    energy[0:4, :] = jnp.zeros((4, 2 * A), jnp.float32)
    energy[4 + A : 8 + A, :] = jnp.zeros((4, 2 * A), jnp.float32)

    for c in range(3):
        for row in range(R):
            prior[0, c, row] = field[c, row + 2, 2 : 2 + W, :]
    leave = pltpu.make_async_copy(prior, displacement, fetched.at[5])
    leave.start()

    def slab(owner):
        return pl.ds(pl.multiple_of(owner * depth, 8), wide)

    def share_copy(step):
        return remote(
            energy.at[slab(peer(step)), :],
            shares.at[load],
            share_send.at[step],
            share_recv.at[step],
            (peer(step), gx, gy),
        )

    each_peer(lambda step: share_copy(step).start())
    shares[load] = energy[slab(load), :]
    each_peer(lambda step: share_copy(step).wait_recv())
    summed = total([shares[index] for index in range(n_load)])
    value = -(2.0 / n_load) * weights[slab(load), :] * summed
    share[...] = value
    share_pack[...] = fold_pack([value[:, 0:A], value[:, A : 2 * A]])

    sides = [share.at[:, pl.ds(0, A)], share.at[:, pl.ds(A, A)]]
    last_around = [
        around(index, beside2, packs2, last_send, last_recv, sides, share_pack)
        for index in range(8)
    ]
    for index, (dx, dy) in enumerate(AROUND):

        @pl.when(inside(dx, dy))
        def _():
            last_around[index].start()

    for index, (dx, dy) in enumerate(AROUND):

        @pl.when(inside(dx, dy))
        def _():
            last_around[opposite[index]].wait_recv()

    lane = lanes((wide, A))
    for row in range(-4, R + 4):
        if row < 0:
            body, pack = beside2[0], 0
        elif row < R:
            body, pack = share[:, A * (row // 4) : A * (row // 4) + A], 1
        else:
            body, pack = beside2[1], 2
        at = row % R
        line = turned(body, 4 - W * (at % 4))
        after = unfolded(packs2[pack, 1], 4 + W - 4 * at)
        before = unfolded(packs2[pack, 0], -64 - 4 * at)
        line = jnp.where(lane < 4, before, line)
        line = jnp.where(lane >= W + 4, after, line)
        line = jnp.where(lane < W + 8, line, 0.0)
        ring_waves[0][row + 4, 8 : 8 + wide, :] = line / theta

    span = slice(8, 8 + wide)
    for sweep, (own_factor, last_factor, near_factor) in enumerate(terms):
        source = ring_waves[sweep]
        for row in range(1 + sweep, 15 - sweep):
            middle = source[row, span, :]
            near = (
                source[row - 1, span, :]
                + source[row + 1, span, :]
                + source[row, 7 : 7 + wide, :]
                + source[row, 9 : 9 + wide, :]
                + pltpu.roll(middle, A - 1, 1)
                + pltpu.roll(middle, 1, 1)
            )
            direction = own_factor * middle + near_factor * near
            if sweep:
                direction = direction + last_factor * ring_waves[sweep - 1][row, span, :]
            ring_waves[sweep + 1][row, span, :] = direction * ring_mask[row]
    for row in range(R):
        summed = total([ref[row + 4, 12 : 12 + depth, :] for ref in ring_waves])
        sensitivity[row] = turned(summed, -4)[:, 0:W]

    leave.wait()
    for index, (dx, dy) in enumerate(AROUND):

        @pl.when(inside(dx, dy))
        def _():
            first_around[index].wait_send()
            last_around[index].wait_send()

    for dx, copy in row_copies + corner_copies:
        pl.when(inside(dx, 0))(copy.wait_send)
    for dy, copy in column_copies:
        pl.when(inside(0, dy))(copy.wait_send)
    each_peer(lambda step: own_copy(step).wait_send())
    each_peer(lambda step: halo_copy(step, 0).wait_send())
    each_peer(lambda step: halo_copy(step, 1).wait_send())
    each_peer(lambda step: share_copy(step).wait_send())


def body(counts, density, displacement_prior, support, load_nodes, load_forces):
    n_load = counts[0]
    depth = A // n_load
    wide = depth + 8
    folded = 8 if wide == 16 else wide
    picks = load_nodes.shape[1]
    real, whole = jnp.float32, jnp.int32
    scratch = [
        ((R, depth, W), real),
        (displacement_prior.shape, real),
        ((R, W, A), whole),
        ((1, picks), whole),
        ((3, 1, picks), real),
        ((R, depth, A), real),
        ((depth, 3 * A), real),
        ((n_load, depth, 2 * A), real),
        ((2, depth, 2 * A), real),
        ((3, 2, depth, A), real),
        ((depth, 6 * A), real),
        ((n_load, depth, 6 * A), real),
        ((24, 64, A), real),
        ((24, 64, A), real),
        ((24, 64, A), real),
        ((24, 64, A), real),
        ((24, 64, A), real),
        ((24, 48, A), real),
        ((12, USED, A), real),
        ((3, 2, W, A), real),
        ((3, 3, W, A), real),
        ((1, W, A), whole),
        ((2, W, A), whole),
        ((11 * R, A), real),
        ((7 * R, A), real),
        ((7 * R, A), real),
        ((11 * R, A), real),
        ((2, 7 * R, A), real),
        ((2, 11 * R, A), real),
        ((3, ROWS, PITCH, A), real),
        ((3, ROWS, PITCH, A), real),
        ((3, ROWS, PITCH, A), real),
        ((12, 8 + USED, A), real),
        ((ROWS, PITCH, A), real),
        ((12, USED, A), real),
        ((11 * USED, 3 * A), real),
        ((8, picks), whole),
        ((A + 8, 2 * A), real),
        ((n_load, wide, 2 * A), real),
        ((A + 8, 2 * A), real),
        ((wide, 2 * A), real),
        ((folded, A), real),
        ((2, wide, A), real),
        ((3, 2, folded, A), real),
        ((16, wide + 16, A), real),
        ((16, wide + 16, A), real),
        ((16, wide + 16, A), real),
        ((16, wide + 16, A), real),
        ((16, wide + 16, A), real),
        ((3, ROWS, PITCH, A), real),
        ((3, ROWS, PITCH, A), real),
        ((3, ROWS, PITCH, A), real),
        ((24, 48, A), real),
        ((16, wide, A), real),
    ]
    semaphores = [8, 8, n_load, n_load, (2, n_load), (2, n_load), 4, 4, 2, 2, 4, 4, n_load, n_load, 8, 8, 6]
    displacement, sensitivity = pl.pallas_call(
        functools.partial(kernel, counts, depth),
        out_shape=(
            jax.ShapeDtypeStruct(displacement_prior.shape, real),
            jax.ShapeDtypeStruct((R, depth, W), real),
        ),
        in_specs=[pl.BlockSpec(memory_space=pltpu.HBM)] * 5,
        out_specs=(pl.BlockSpec(memory_space=pltpu.HBM), pl.BlockSpec(memory_space=pltpu.VMEM)),
        scratch_shapes=[pltpu.VMEM(shape, kind) for shape, kind in scratch]
        + [pltpu.SemaphoreType.DMA(count if isinstance(count, tuple) else (count,)) for count in semaphores],
        compiler_params=pltpu.CompilerParams(
            collective_id=0, has_side_effects=True, vmem_limit_bytes=67_043_328
        ),
        name="elasticity",
    )(
        jnp.transpose(density, (0, 2, 1)),
        displacement_prior,
        support,
        load_nodes,
        jnp.transpose(load_forces, (1, 0, 2)),
    )
    return displacement, jnp.transpose(sensitivity, (0, 2, 1))


def solution(mesh):
    counts = tuple(mesh.shape[axis] for axis in ("load", "gx", "gy"))
    return jax.shard_map(
        functools.partial(body, counts),
        mesh=mesh,
        in_specs=(
            P("gx", "gy", "load"),
            P("load", None, "gx", "gy", None),
            P("gx", "gy", None),
            P("load", None),
            P("load", None, None),
        ),
        out_specs=(P("load", None, "gx", "gy", None), P("gx", "gy", "load")),
        check_vma=False,
    )
```

```python
import functools

import jax
import jax.numpy as jnp
from jax import lax
from jax.experimental import pallas as pl
from jax.experimental.pallas import tpu as pltpu
from jax.sharding import PartitionSpec as P

SWEEPS = 4
JACOBI = 2

poisson_ratio = 0.3
filter_weight = 3.0
relax_factor = 0.6
modulus_floor = 0.05
lame = poisson_ratio / ((1 + poisson_ratio) * (1 - 2 * poisson_ratio))
shear = 1.0 / (2 * (1 + poisson_ratio))

R = 8
W = 32
A = 128
N = 3 * R * W
ROWS = 13
PITCH = 48
USED = 40
BLOCKS = USED // 8
CHUNK = 512
MESH = pl.DeviceIdType.MESH
AROUND = [(-1, -1), (-1, 1), (1, -1), (1, 1), (0, -1), (0, 1), (-1, 0), (1, 0)]


def chebyshev_factors():
    theta = 1.0 + 6.0 * filter_weight
    delta = 6.0 * filter_weight
    sigma = theta / delta
    ratio = 1.0 / sigma
    steps = []
    for _ in range(SWEEPS):
        following = 1.0 / (2.0 * sigma - ratio)
        steps.append((following * ratio, 2.0 * following / delta))
        ratio = following
    return theta, steps


def chebyshev_terms():
    theta, steps = chebyshev_factors()
    terms = []
    before = None
    for keep, gain in steps:
        own, last = keep - gain * theta, 0.0
        if before is None:
            own += gain * theta
        else:
            own += gain / before[1]
            last = -gain / before[1] * before[0]
        terms.append((own, last, gain * filter_weight))
        before = keep, gain
    return theta, terms


def lanes(shape):
    return lax.broadcasted_iota(jnp.int32, shape, len(shape) - 1)


def lane_up(x):
    return jnp.where(lanes(x.shape) == A - 1, 0.0, pltpu.roll(x, A - 1, x.ndim - 1))


def lane_down(x):
    return jnp.where(lanes(x.shape) == 0, 0.0, pltpu.roll(x, 1, x.ndim - 1))


def fold_pack(halves):
    wide = halves[0].shape[0]
    lane = lanes((wide, A))
    packed = jnp.zeros((wide, A), jnp.float32)
    for row in range(R):
        at = W * (row % 4)
        for start, column in ((4 * row, 0), (64 + 4 * row, W - 4)):
            moved = turned(halves[row // 4], start - at - column)
            packed = jnp.where((lane >= start) & (lane < start + 4), moved, packed)
    if wide != 16:
        return packed
    lane = lanes((8, A))
    return jnp.where((lane & 32) == 0, packed[0:8], turned(packed[8:16], 32))


def unfolded(pack, steps):
    if pack.shape[0] != 8:
        return turned(pack, steps)
    return jnp.concatenate([turned(pack, steps), turned(pack, steps - 32)], axis=0)


def turned(x, steps):
    steps %= A
    return pltpu.roll(x, steps, 1) if steps else x


def edge_pack(halves):
    lane = lanes(halves[0].shape)
    packed = jnp.zeros(halves[0].shape, jnp.float32)
    for row in range(R):
        at = W * (row % 4)
        for start, column in ((8 * row, 0), (64 + 8 * row, W - 8)):
            moved = turned(halves[row // 4], start - at - column)
            packed = jnp.where((lane >= start) & (lane < start + 8), moved, packed)
    return packed


def peers_of(count):
    side = 4 if count == 16 else count
    steps = [(a, b) for a in range(count // side) for b in range(side)][1:]

    def hops(step):
        return min(step[0], count // side - step[0]) + min(step[1], side - step[1])

    return side, sorted(steps, key=hops, reverse=True)


def total(values):
    result = values[0]
    for value in values[1:]:
        result = result + value
    return result


def groups():
    return [
        ([(0, 1, 0, 0), (1, 0, 1, 0), (2, 0, 0, 1)], lame / 16, 2 * shear / 16),
        ([(0, 0, 1, 0), (1, 1, 0, 0)], shear / 16, None),
        ([(0, 0, 0, 1), (2, 1, 0, 0)], shear / 16, None),
        ([(1, 0, 0, 1), (2, 0, 1, 0)], shear / 16, None),
        ([(0, 0, 1, 1), (1, 1, 0, 1), (2, 1, 1, 0)], shear / 48, shear / 48),
        ([(0, 1, 0, 1), (1, 0, 1, 1)], lame / 48, 3 * shear / 48),
        ([(0, 1, 1, 0), (2, 0, 1, 1)], lame / 48, 3 * shear / 48),
        ([(1, 1, 1, 0), (2, 1, 0, 1)], lame / 48, 3 * shear / 48),
        ([(0, 1, 1, 1)], None, (lame + 4 * shear) / 144),
        ([(1, 1, 1, 1)], None, (lame + 4 * shear) / 144),
        ([(2, 1, 1, 1)], None, (lame + 4 * shear) / 144),
    ]


def element_forces(coefs, modulus):
    scaled = {}

    def times(weight, value):
        if weight not in scaled:
            scaled[weight] = modulus * weight
        return scaled[weight] * value

    forces = {}
    for members, joint, single in groups():
        if joint is not None:
            common = total([coefs[m] for m in members])
            if joint == single:
                for m in members:
                    forces[m] = times(joint, common + coefs[m])
                continue
            common = times(joint, common)
            for m in members:
                forces[m] = common if single is None else common + times(single, coefs[m])
        else:
            for m in members:
                forces[m] = times(single, coefs[m])
    return forces


def element_energy(coefs):
    terms = {}
    for members, joint, single in groups():
        if joint is not None:
            common = total([coefs[m] for m in members])
            terms.setdefault(joint, []).append(common * common)
        if single is not None:
            for m in members:
                terms.setdefault(single, []).append(coefs[m] * coefs[m])
    return total([weight * total(values) for weight, values in terms.items()])


def plane_sums(field, lifted, row, column):
    out = {}
    for c in range(3):
        near = field[c, row, pl.ds(column, 8), :]
        far = field[c, row, pl.ds(column + 1, 8), :]
        near_up = lifted[c, row, pl.ds(column, 8), :]
        far_up = lifted[c, row, pl.ds(column + 1, 8), :]
        for q, value, up in ((0, near + far, near_up + far_up), (1, far - near, far_up - near_up)):
            out[c, q, 0] = value + up
            out[c, q, 1] = up - value
    return out


def in_groups(first, last, size, action, carry=0):
    trips = (last - first) // size

    def trip(index, carry):
        for at in range(size):
            carry = action(first + index * size + at, carry)
        return carry

    if trips > 1:
        carry = lax.fori_loop(0, trips, trip, carry)
        first += trips * size
    for row in range(first, last):
        carry = action(row, carry)
    return carry


KEYS = [(c, q, r) for c in range(3) for q in range(2) for r in range(2)]


def row_coefs(low, high):
    coefs = {}
    for c, q, r in KEYS:
        coefs[c, 0, q, r] = low[c, q, r] + high[c, q, r]
        coefs[c, 1, q, r] = high[c, q, r] - low[c, q, r]
    return coefs


def kernel(
    counts,
    depth,
    density_in,
    prior_in,
    support_in,
    nodes_in,
    forces_in,
    displacement,
    sensitivity,
    density,
    prior,
    support,
    load_nodes,
    load_forces,
    raw,
    own,
    tile,
    beside,
    packs,
    halo,
    halos,
    wave0,
    wave1,
    wave2,
    wave3,
    wave4,
    remain,
    result,
    rows_low,
    rows_high,
    fixed_low,
    fixed_high,
    send_low,
    send_high,
    columns_low,
    columns_high,
    corners_low,
    corners_high,
    field,
    near_part,
    far_part,
    modulus,
    free,
    step_size,
    force,
    spread,
    energy,
    shares,
    weights,
    share,
    share_pack,
    beside2,
    packs2,
    ring_wave0,
    ring_wave1,
    ring_wave2,
    ring_wave3,
    ring_wave4,
    lifted,
    near_upper,
    far_upper,
    mask,
    ring_mask,
    around_send,
    around_recv,
    own_send,
    own_recv,
    halo_send,
    halo_recv,
    rows_send,
    rows_recv,
    column_send,
    column_recv,
    corner_send,
    corner_recv,
    share_send,
    share_recv,
    last_send,
    last_recv,
    fetched,
):
    n_load, n_x, n_y = counts
    waves = [wave0, wave1, wave2, wave3, wave4]
    wave = wave0
    ring_waves = [ring_wave0, ring_wave1, ring_wave2, ring_wave3, ring_wave4]
    wide = depth + 8
    load, gx, gy = lax.axis_index("load"), lax.axis_index("gx"), lax.axis_index("gy")

    def inside(dx, dy):
        return (gx + dx >= 0) & (gx + dx < n_x) & (gy + dy >= 0) & (gy + dy < n_y)

    side, steps = peers_of(n_load)

    def peer(step):
        a, b = steps[step]
        across = lax.rem(lax.div(load, side) + a, n_load // side)
        return across * side + lax.rem(lax.rem(load, side) + b, side)

    def each_peer(action):
        for step in range(n_load - 1):
            action(step)

    def remote(src, dst, send, recv, where):
        return pltpu.make_async_remote_copy(
            src_ref=src,
            dst_ref=dst,
            send_sem=send,
            recv_sem=recv,
            device_id=where,
            device_id_type=MESH,
        )

    def toward(dx, dy):
        return (load, gx + dx, gy + dy)

    barrier = pltpu.get_barrier_semaphore()
    each_peer(
        lambda step: pl.semaphore_signal(
            barrier, inc=1, device_id=(peer(step), gx, gy), device_id_type=MESH
        )
    )
    expected = n_load - 1
    for dx, dy in AROUND:
        expected = expected + inside(dx, dy).astype(jnp.int32)

        @pl.when(inside(dx, dy))
        def _():
            pl.semaphore_signal(
                barrier, inc=1, device_id=toward(dx, dy), device_id_type=MESH
            )

    fetches = [
        pltpu.make_async_copy(source, target, fetched.at[index])
        for index, (source, target) in enumerate(
            (
                (density_in, density),
                (prior_in, prior),
                (support_in, support),
                (nodes_in, load_nodes),
                (forces_in, load_forces),
            )
        )
    ]
    for fetch in fetches:
        fetch.start()

    fetches[0].wait()
    for row in range(R):
        raw[row, :, 0:W] = density[row]
    halves = []
    for half in range(2):
        value = jnp.zeros((depth, A), jnp.float32)
        lane = lanes(value.shape)
        for row in range(4):
            moved = turned(raw[4 * half + row], W * row)
            value = jnp.where((lane >= W * row) & (lane < W * row + W), moved, value)
        halves.append(value)
        own[:, A * half : A * half + A] = value
        tile[load, :, A * half : A * half + A] = value
    own[:, 2 * A : 3 * A] = edge_pack(halves)

    fetches[1].wait()
    fetches[2].wait()

    for row in range(R):
        for c in range(3):
            send_low[11 * row + 3 * c : 11 * row + 3 * c + 3, :] = prior[0, c, row, 0:3, :]
            send_high[7 * row + 2 * c : 7 * row + 2 * c + 2, :] = prior[0, c, row, W - 2 : W, :]
        send_low[11 * row + 9 : 11 * row + 11, :] = support[row, 0:2, :].astype(jnp.float32)
        send_high[7 * row + 6 : 7 * row + 7, :] = support[row, W - 1 : W, :].astype(jnp.float32)

    pl.semaphore_wait(barrier, expected)

    def around(index, whole, narrow, send, recv, sources, pack):
        dx, dy = AROUND[index]
        if dy == 0:
            return remote(
                sources[(1 + dx) // 2], whole.at[(1 - dx) // 2], send.at[index], recv.at[index], toward(dx, dy)
            )
        return remote(
            pack, narrow.at[1 - dx, (1 - dy) // 2], send.at[index], recv.at[index], toward(dx, dy)
        )

    first_around = [
        around(
            index,
            beside,
            packs,
            around_send,
            around_recv,
            [own.at[:, pl.ds(0, 2 * A)]] * 2,
            own.at[:, pl.ds(2 * A, A)],
        )
        for index in range(8)
    ]
    opposite = [AROUND.index((-dx, -dy)) for dx, dy in AROUND]

    for index, (dx, dy) in enumerate(AROUND):

        @pl.when(inside(dx, dy))
        def _():
            first_around[index].start()

    def own_copy(step):
        return remote(
            own.at[:, pl.ds(0, 2 * A)],
            tile.at[load],
            own_send.at[step],
            own_recv.at[step],
            (peer(step), gx, gy),
        )

    each_peer(lambda step: own_copy(step).start())

    row_copies = [
        (-1, remote(prior_in.at[0, :, pl.ds(0, 3)], rows_high, rows_send.at[0], rows_recv.at[0], toward(-1, 0))),
        (-1, remote(support_in.at[pl.ds(0, 2)], fixed_high, rows_send.at[1], rows_recv.at[1], toward(-1, 0))),
        (1, remote(prior_in.at[0, :, pl.ds(R - 2, 2)], rows_low, rows_send.at[2], rows_recv.at[2], toward(1, 0))),
        (1, remote(support_in.at[pl.ds(R - 1, 1)], fixed_low, rows_send.at[3], rows_recv.at[3], toward(1, 0))),
    ]
    column_copies = [
        (-1, remote(send_low, columns_high, column_send.at[0], column_recv.at[0], toward(0, -1))),
        (1, remote(send_high, columns_low, column_send.at[1], column_recv.at[1], toward(0, 1))),
    ]
    for dy, copy in column_copies:
        pl.when(inside(0, dy))(copy.start)
    for dx, copy in row_copies:
        pl.when(inside(dx, 0))(copy.start)

    for index, (dx, dy) in enumerate(AROUND):

        @pl.when(jnp.logical_not(inside(dx, dy)))
        def _():
            if dy == 0:
                for ref in (beside, beside2):
                    ref[(dx + 1) // 2] = jnp.zeros(ref.shape[1:], jnp.float32)
            else:
                for ref in (packs, packs2):
                    ref[dx + 1, (dy + 1) // 2] = jnp.zeros(ref.shape[2:], jnp.float32)

    @pl.when(jnp.logical_not(inside(-1, 0)))
    def _():
        rows_low[...] = jnp.zeros(rows_low.shape, jnp.float32)
        fixed_low[...] = jnp.zeros(fixed_low.shape, jnp.int32)
        corners_low[0] = jnp.zeros(corners_low.shape[1:], jnp.float32)
        corners_high[0] = jnp.zeros(corners_high.shape[1:], jnp.float32)

    @pl.when(jnp.logical_not(inside(1, 0)))
    def _():
        rows_high[...] = jnp.zeros(rows_high.shape, jnp.float32)
        fixed_high[...] = jnp.zeros(fixed_high.shape, jnp.int32)
        corners_low[1] = jnp.zeros(corners_low.shape[1:], jnp.float32)
        corners_high[1] = jnp.zeros(corners_high.shape[1:], jnp.float32)

    @pl.when(jnp.logical_not(inside(0, -1)))
    def _():
        columns_low[...] = jnp.zeros(columns_low.shape, jnp.float32)

    @pl.when(jnp.logical_not(inside(0, 1)))
    def _():
        columns_high[...] = jnp.zeros(columns_high.shape, jnp.float32)


    def in_grid(row, columns):
        row, columns = row + gx * R, columns + gy * W
        return (row >= 0) & (row < n_x * R) & (columns >= 0) & (columns < n_y * W)

    def halo_copy(step, part):
        span = pl.ds(part * 3 * A, 3 * A)
        return remote(
            halo.at[:, span],
            halos.at[load, :, span],
            halo_send.at[part, step],
            halo_recv.at[part, step],
            (peer(step), gx, gy),
        )

    for index, (dx, dy) in enumerate(AROUND):
        if dy == 0:

            @pl.when(inside(dx, dy))
            def _():
                first_around[opposite[index]].wait_recv()

    lane = lanes((depth, A))
    halo[:, 0:A] = beside[0, :, A : 2 * A]
    halo[:, A : 2 * A] = beside[1, :, 0:A]
    halo[:, 2 * A : 3 * A] = jnp.where(lane < 64, beside[1, :, A : 2 * A], beside[0, :, 0:A])
    halos[load, :, 0 : 3 * A] = halo[:, 0 : 3 * A]
    each_peer(lambda step: halo_copy(step, 0).start())

    fetches[3].wait()
    fetches[4].wait()
    flat = load_nodes[...]
    column_bits = (n_y * W).bit_length() - 1
    node_row = lax.shift_right_logical(flat, 7 + column_bits) - gx * R + 1
    node_column = (lax.shift_right_logical(flat, 7) & (n_y * W - 1)) - gy * W + 2
    held = (node_row >= 0) & (node_row < 11) & (node_column >= 0) & (node_column < USED)
    spread[0:1, :] = jnp.where(held, node_row * USED + node_column, -1)
    spread[1:2, :] = flat & (A - 1)
    force[...] = jnp.zeros(force.shape, jnp.float32)

    def add_loads(index, carry):
        span = pl.ds(pl.multiple_of(index * CHUNK, CHUNK), CHUNK)
        place = spread[0:1, span]
        depth_of = spread[1:2, span]
        left = jnp.where(
            lax.broadcasted_iota(jnp.int32, (11 * USED, CHUNK), 0) == place, 1.0, 0.0
        ).astype(jnp.bfloat16)
        here = lax.broadcasted_iota(jnp.int32, (A, CHUNK), 0) == depth_of
        rest = [load_forces[c, :, span] for c in range(3)]
        for part in range(3):
            rights = []
            for c in range(3):
                rounded = rest[c].astype(jnp.bfloat16).astype(jnp.float32)
                rest[c] = rest[c] - rounded
                rights.append(jnp.where(here, rounded, 0.0).astype(jnp.bfloat16))
            force[...] += lax.dot_general(
                left,
                jnp.concatenate(rights, axis=0),
                (((1,), (1,)), ((), ())),
                preferred_element_type=jnp.float32,
            )
        return carry

    chunks = load_nodes.shape[1] // CHUNK
    lax.fori_loop(0, chunks // 2, add_loads, 0)

    for index, (dx, dy) in enumerate(AROUND):
        if dy != 0:

            @pl.when(inside(dx, dy))
            def _():
                first_around[opposite[index]].wait_recv()

    for index in range(3):
        at = (3 + index) * A
        halo[:, at : at + A] = jnp.where(lane < 64, packs[index, 1], packs[index, 0])
        halos[load, :, at : at + A] = halo[:, at : at + A]
    each_peer(lambda step: halo_copy(step, 1).start())

    for dy, copy in column_copies:
        other = column_copies[0][1] if dy == 1 else column_copies[1][1]
        pl.when(inside(0, dy))(other.wait_recv)
    corner_copies = []
    for dx in (-1, 1):
        for part, (source, target) in enumerate(
            ((columns_low, corners_low), (columns_high, corners_high))
        ):
            at = (dx + 1) + part
            corner_copies.append(
                (
                    dx,
                    remote(
                        source,
                        target.at[(1 - dx) // 2],
                        corner_send.at[at],
                        corner_recv.at[at],
                        toward(dx, 0),
                    ),
                )
            )
    for dx, copy in corner_copies:
        pl.when(inside(dx, 0))(copy.start)

    lax.fori_loop(chunks // 2, chunks, add_loads, 0)

    def set_mask(row, carry):
        columns = lax.broadcasted_iota(jnp.int32, (48, A), 0) - 8
        mask[row] = jnp.where(in_grid(row - 8, columns), 1.0, 0.0)
        return carry

    in_groups(3, 21, 3, set_mask)

    def set_ring_mask(row, carry):
        lane = lanes((wide, A))
        layer = lax.broadcasted_iota(jnp.int32, (wide, A), 0) - 4 + load * depth
        kept = in_grid(row - 4, lane - 4) & (layer >= 0) & (layer < A) & (lane < W + 8)
        ring_mask[row] = jnp.where(kept, 1.0, 0.0)
        return carry

    in_groups(1, 15, 7, set_ring_mask)

    for c in range(3):
        for row in range(R):
            field[c, row + 2, 2 : 2 + W, :] = prior[0, c, row]
    for row in range(R):
        free[row + 2, 2 : 2 + W, :] = support[row].astype(jnp.float32)

    for dx, copy in row_copies + corner_copies:
        opposite_copy = {
            id(a[1]): b[1]
            for pairs in (
                (row_copies[0], row_copies[2]),
                (row_copies[1], row_copies[3]),
                (corner_copies[0], corner_copies[2]),
                (corner_copies[1], corner_copies[3]),
            )
            for a, b in (pairs, pairs[::-1])
        }[id(copy)]
        pl.when(inside(dx, 0))(opposite_copy.wait_recv)

    for c in range(3):
        for row in range(2):
            field[c, row, 2 : 2 + W, :] = rows_low[c, row]
        for row in range(3):
            field[c, row + 10, 2 : 2 + W, :] = rows_high[c, row]
    free[1, 2 : 2 + W, :] = fixed_low[0].astype(jnp.float32)
    for row in range(2):
        free[row + 10, 2 : 2 + W, :] = fixed_high[row].astype(jnp.float32)
    for row in range(-2, R + 3):
        if row < 0:
            low, high, at = corners_low.at[0], corners_high.at[0], row + R
        elif row < R:
            low, high, at = columns_low, columns_high, row
        else:
            low, high, at = corners_low.at[1], corners_high.at[1], row - R
        for c in range(3):
            field[c, row + 2, 0:2, :] = low[7 * at + 2 * c : 7 * at + 2 * c + 2, :]
            field[c, row + 2, 2 + W : 5 + W, :] = high[11 * at + 3 * c : 11 * at + 3 * c + 3, :]
        free[row + 2, 1:2, :] = low[7 * at + 6 : 7 * at + 7, :]
        free[row + 2, 2 + W : 4 + W, :] = high[11 * at + 9 : 11 * at + 11, :]

    def set_free(row, carry):
        columns = lax.broadcasted_iota(jnp.int32, (PITCH, A), 0) - 2
        kept = in_grid(row - 2, columns) & (columns >= -1) & (columns <= W + 1)
        free[row] = jnp.where(kept & (free[row] == 0.0), 1.0, 0.0)
        return carry

    in_groups(1, 12, 4, set_free)

    def lift(row, carry):
        for c in range(3):
            lifted[c, row] = lane_up(field[c, row])
        return carry

    in_groups(0, ROWS, 4, lift)

    def place(block, pieces):
        value = block.T
        for start, rows, columns, row, column in pieces:
            part = value[start : start + rows * columns].reshape(rows, columns, A)
            wave[row + 8 : row + 8 + rows, column + 16 : column + 16 + columns, :] = part

    each_peer(lambda step: own_copy(step).wait_recv())
    for half in range(2):
        place(tile[:, :, A * half : A * half + A].reshape(A, A), [(0, 4, W, 4 * half, 0)])
    layout = [
        [(0, 4, W, -4, 0)],
        [(0, 4, W, 8, 0)],
        [(0, 2, W, 12, 0), (64, 2, W, -6, 0)],
    ] + [[(0, 8, 8, dx * R, W), (64, 8, 8, dx * R, -8)] for dx in (-1, 0, 1)]
    for index, pieces in enumerate(layout):
        if index % 3 == 0:
            each_peer(lambda step: halo_copy(step, index // 3).wait_recv())
        place(halos[:, :, A * index : A * index + A].reshape(A, A), pieces)

    theta, terms = chebyshev_terms()

    def start_filter(row, carry):
        wave[row, 8:56, :] = wave[row, 8:56, :] / theta
        return carry

    in_groups(2, 22, 5, start_filter)
    for sweep, (own_factor, last_factor, near_factor) in enumerate(terms):

        def one_row(row, carry, source=waves[sweep], target=waves[sweep + 1]):
            middle = source[row, 8:56, :]
            near = (
                source[row - 1, 8:56, :]
                + source[row + 1, 8:56, :]
                + source[row, 7:55, :]
                + source[row, 9:57, :]
                + lane_up(middle)
                + lane_down(middle)
            )
            direction = own_factor * middle + near_factor * near
            if sweep:
                direction = direction + last_factor * waves[sweep - 1][row, 8:56, :]
            target[row, 8:56, :] = direction * mask[row]
            return carry

        in_groups(3 + sweep, 21 - sweep, 3, one_row)

    def set_modulus(row, carry):
        filtered = total([ref[row + 6, 14 : 14 + USED, :] for ref in waves])
        result[row] = filtered
        columns = lax.broadcasted_iota(jnp.int32, (USED, A), 0) - 2
        modulus[row, 0:8, :] = jnp.zeros((8, A), jnp.float32)
        modulus[row, 8 : 8 + USED, :] = jnp.where(
            in_grid(row - 2, columns), modulus_floor + filtered * filtered, 0.0
        )
        return carry

    in_groups(0, 12, 3, set_modulus)
    for half in range(2):
        tall = result[2 + 4 * half : 6 + 4 * half, 2 : 2 + W, :].reshape(A, A)
        weights[4 : 4 + A, A * half : A * half + A] = tall.T
    weights[0:4, :] = jnp.zeros((4, 2 * A), jnp.float32)
    weights[4 + A : 8 + A, :] = jnp.zeros((4, 2 * A), jnp.float32)

    def set_step(row, carry):
        around_node = total(
            [modulus[row - 1 + p, 7 + q : 7 + q + USED, :] for p in range(2) for q in range(2)]
        )
        around_node = around_node + lane_down(around_node)
        step_size[row] = relax_factor / ((lame + 4 * shear) / 9 * around_node)
        return carry

    in_groups(1, 12, 4, set_step)

    for sweep in range(JACOBI):
        first, last = 1 + sweep, 12 - sweep
        for block in range(BLOCKS):

            def one_element_row(row, carry, column=8 * block):
                low, pending = carry
                low = dict(zip(KEYS, low))
                high = plane_sums(field, lifted, row + 1, column)
                forces = element_forces(
                    row_coefs(low, high), modulus[row, pl.ds(column + 8, 8), :]
                )
                node = {}
                following = []
                for at, (c, q, r) in enumerate(KEYS):
                    change = forces[c, 1, q, r]
                    if (c, 0, q, r) in forces:
                        same = forces[c, 0, q, r]
                        node[c, q, r] = pending[at] + (same - change)
                        following.append(same + change)
                    else:
                        node[c, q, r] = pending[at] - change
                        following.append(change)
                for c in range(3):
                    for sign, near_to, far_to in (
                        (-1, near_part, far_part),
                        (1, near_upper, far_upper),
                    ):
                        sums, changes = (
                            node[c, q, 0] + node[c, q, 1] if sign > 0 else node[c, q, 0] - node[c, q, 1]
                            for q in range(2)
                        )
                        near_to[c, row, pl.ds(column, 8), :] = sums - changes
                        far_to[c, row, pl.ds(column + 1, 8), :] = sums + changes
                return [high[key] for key in KEYS], following

            low = plane_sums(field, lifted, first - 1, 8 * block)
            nothing = [jnp.zeros((8, A), jnp.float32)] * len(KEYS)
            in_groups(
                first - 1,
                last,
                (last - first + 1) // 2,
                one_element_row,
                ([low[key] for key in KEYS], nothing),
            )

        def one_node_row(row, carry):
            span = pl.ds(0, USED)
            rate = step_size[row]
            open_here = free[row, span, :] > 0.0
            for c in range(3):
                applied = near_part[c, row, span, :] + far_part[c, row, span, :]
                applied = applied + lane_down(near_upper[c, row, span, :] + far_upper[c, row, span, :])
                load_here = force[pl.ds(pl.multiple_of((row - 1) * USED, 8), USED), A * c : A * c + A]
                moved = field[c, row, span, :] + (load_here - applied) * rate
                moved = jnp.where(open_here, moved, 0.0)
                field[c, row, span, :] = moved
                lifted[c, row, span, :] = lane_up(moved)
            return carry

        in_groups(first, last, 2, one_node_row)

    for block in range(W // 8):

        def one_energy_row(row, low, column=8 * block + 2):
            high = plane_sums(field, lifted, row + 1, column)
            value = element_energy(row_coefs(dict(zip(KEYS, low)), high))
            remain[row, pl.ds(column - 2, 8), :] = value
            return [high[key] for key in KEYS]

        low = plane_sums(field, lifted, 2, 8 * block + 2)
        in_groups(2, 10, 4, one_energy_row, [low[key] for key in KEYS])
    for half in range(2):
        tall = remain[2 + 4 * half : 6 + 4 * half, 0:W, :].reshape(A, A)
        energy[4 : 4 + A, A * half : A * half + A] = tall.T
    energy[0:4, :] = jnp.zeros((4, 2 * A), jnp.float32)
    energy[4 + A : 8 + A, :] = jnp.zeros((4, 2 * A), jnp.float32)

    def slab(owner):
        return pl.ds(pl.multiple_of(owner * depth, 8), wide)

    def share_copy(step):
        return remote(
            energy.at[slab(peer(step)), :],
            shares.at[step],
            share_send.at[step],
            share_recv.at[step],
            (peer(step), gx, gy),
        )

    each_peer(lambda step: share_copy(step).start())
    for c in range(3):
        for row in range(R):
            displacement[0, c, row] = field[c, row + 2, 2 : 2 + W, :]

    scale = -(2.0 / n_load) * weights[slab(load), :]
    each_peer(lambda step: share_copy(step).wait_recv())
    value = energy[slab(load), :]
    for step in range(n_load - 1):
        value = value + shares[step]
    value = scale * value
    share[...] = value
    share_pack[...] = fold_pack([value[:, 0:A], value[:, A : 2 * A]])

    sides = [share.at[:, pl.ds(0, A)], share.at[:, pl.ds(A, A)]]
    last_around = [
        around(index, beside2, packs2, last_send, last_recv, sides, share_pack)
        for index in range(8)
    ]
    for index, (dx, dy) in enumerate(AROUND):

        @pl.when(inside(dx, dy))
        def _():
            last_around[index].start()

    for index, (dx, dy) in enumerate(AROUND):

        @pl.when(inside(dx, dy))
        def _():
            last_around[opposite[index]].wait_recv()

    lane = lanes((wide, A))
    for row in range(-4, R + 4):
        if row < 0:
            body, pack = beside2[0], 0
        elif row < R:
            body, pack = share[:, A * (row // 4) : A * (row // 4) + A], 1
        else:
            body, pack = beside2[1], 2
        at = row % R
        line = turned(body, 4 - W * (at % 4))
        after = unfolded(packs2[pack, 1], 4 + W - 4 * at)
        before = unfolded(packs2[pack, 0], -64 - 4 * at)
        line = jnp.where(lane < 4, before, line)
        line = jnp.where(lane >= W + 4, after, line)
        line = jnp.where(lane < W + 8, line, 0.0)
        ring_waves[0][row + 4, 8 : 8 + wide, :] = line / theta

    span = slice(8, 8 + wide)
    for sweep, (own_factor, last_factor, near_factor) in enumerate(terms):
        source = ring_waves[sweep]
        for row in range(1 + sweep, 15 - sweep):
            middle = source[row, span, :]
            near = (
                source[row - 1, span, :]
                + source[row + 1, span, :]
                + source[row, 7 : 7 + wide, :]
                + source[row, 9 : 9 + wide, :]
                + pltpu.roll(middle, A - 1, 1)
                + pltpu.roll(middle, 1, 1)
            )
            direction = own_factor * middle + near_factor * near
            if sweep:
                direction = direction + last_factor * ring_waves[sweep - 1][row, span, :]
            ring_waves[sweep + 1][row, span, :] = direction * ring_mask[row]
    for row in range(R):
        summed = total([ref[row + 4, 12 : 12 + depth, :] for ref in ring_waves])
        sensitivity[row] = turned(summed, -4)[:, 0:W]

    for index, (dx, dy) in enumerate(AROUND):

        @pl.when(inside(dx, dy))
        def _():
            first_around[index].wait_send()
            last_around[index].wait_send()

    for dx, copy in row_copies + corner_copies:
        pl.when(inside(dx, 0))(copy.wait_send)
    for dy, copy in column_copies:
        pl.when(inside(0, dy))(copy.wait_send)
    each_peer(lambda step: own_copy(step).wait_send())
    each_peer(lambda step: halo_copy(step, 0).wait_send())
    each_peer(lambda step: halo_copy(step, 1).wait_send())
    each_peer(lambda step: share_copy(step).wait_send())


def body(counts, density, displacement_prior, support, load_nodes, load_forces):
    n_load = counts[0]
    depth = A // n_load
    wide = depth + 8
    folded = 8 if wide == 16 else wide
    picks = load_nodes.shape[1]
    real, whole = jnp.float32, jnp.int32
    scratch = [
        ((R, depth, W), real),
        (displacement_prior.shape, real),
        ((R, W, A), whole),
        ((1, picks), whole),
        ((3, 1, picks), real),
        ((R, depth, A), real),
        ((depth, 3 * A), real),
        ((n_load, depth, 2 * A), real),
        ((2, depth, 2 * A), real),
        ((3, 2, depth, A), real),
        ((depth, 6 * A), real),
        ((n_load, depth, 6 * A), real),
        ((24, 64, A), real),
        ((24, 64, A), real),
        ((24, 64, A), real),
        ((24, 64, A), real),
        ((24, 64, A), real),
        ((24, 48, A), real),
        ((12, USED, A), real),
        ((3, 2, W, A), real),
        ((3, 3, W, A), real),
        ((1, W, A), whole),
        ((2, W, A), whole),
        ((11 * R, A), real),
        ((7 * R, A), real),
        ((7 * R, A), real),
        ((11 * R, A), real),
        ((2, 7 * R, A), real),
        ((2, 11 * R, A), real),
        ((3, ROWS, PITCH, A), real),
        ((3, ROWS, PITCH, A), real),
        ((3, ROWS, PITCH, A), real),
        ((12, 8 + USED, A), real),
        ((ROWS, PITCH, A), real),
        ((12, USED, A), real),
        ((11 * USED, 3 * A), real),
        ((8, picks), whole),
        ((A + 8, 2 * A), real),
        ((n_load, wide, 2 * A), real),
        ((A + 8, 2 * A), real),
        ((wide, 2 * A), real),
        ((folded, A), real),
        ((2, wide, A), real),
        ((3, 2, folded, A), real),
        ((16, wide + 16, A), real),
        ((16, wide + 16, A), real),
        ((16, wide + 16, A), real),
        ((16, wide + 16, A), real),
        ((16, wide + 16, A), real),
        ((3, ROWS, PITCH, A), real),
        ((3, ROWS, PITCH, A), real),
        ((3, ROWS, PITCH, A), real),
        ((24, 48, A), real),
        ((16, wide, A), real),
    ]
    semaphores = [8, 8, n_load, n_load, (2, n_load), (2, n_load), 4, 4, 2, 2, 4, 4, n_load, n_load, 8, 8, 5]
    displacement, sensitivity = pl.pallas_call(
        functools.partial(kernel, counts, depth),
        out_shape=(
            pltpu.VMEM(displacement_prior.shape, real),
            pltpu.VMEM((R, depth, W), real),
        ),
        in_specs=[pl.BlockSpec(memory_space=pltpu.HBM)] * 5,
        out_specs=(pl.BlockSpec(memory_space=pltpu.VMEM),) * 2,
        scratch_shapes=[pltpu.VMEM(shape, kind) for shape, kind in scratch]
        + [pltpu.SemaphoreType.DMA(count if isinstance(count, tuple) else (count,)) for count in semaphores],
        compiler_params=pltpu.CompilerParams(
            collective_id=0, has_side_effects=True, vmem_limit_bytes=67_043_328 - (1 << 19),
        ),
        name="elasticity",
    )(
        jnp.transpose(density, (0, 2, 1)),
        displacement_prior,
        support,
        load_nodes,
        jnp.transpose(load_forces, (1, 0, 2)),
    )
    return displacement, jnp.transpose(sensitivity, (0, 2, 1))


def solution(mesh):
    counts = tuple(mesh.shape[axis] for axis in ("load", "gx", "gy"))
    return jax.shard_map(
        functools.partial(body, counts),
        mesh=mesh,
        in_specs=(
            P("gx", "gy", "load"),
            P("load", None, "gx", "gy", None),
            P("gx", "gy", None),
            P("load", None),
            P("load", None, None),
        ),
        out_specs=(P("load", None, "gx", "gy", None), P("gx", "gy", "load")),
        check_vma=False,
    )
```

```python
import functools

import jax
import jax.numpy as jnp
from jax import lax
from jax.experimental import pallas as pl
from jax.experimental.pallas import tpu as pltpu
from jax.sharding import PartitionSpec as P

SWEEPS = 4
JACOBI = 2

poisson_ratio = 0.3
filter_weight = 3.0
relax_factor = 0.6
modulus_floor = 0.05
lame = poisson_ratio / ((1 + poisson_ratio) * (1 - 2 * poisson_ratio))
shear = 1.0 / (2 * (1 + poisson_ratio))

R = 8
W = 32
A = 128
N = 3 * R * W
ROWS = 13
PITCH = 48
USED = 40
BLOCKS = USED // 8
CHUNK = 512
MESH = pl.DeviceIdType.MESH
AROUND = [(-1, -1), (-1, 1), (1, -1), (1, 1), (0, -1), (0, 1), (-1, 0), (1, 0)]


def chebyshev_factors():
    theta = 1.0 + 6.0 * filter_weight
    delta = 6.0 * filter_weight
    sigma = theta / delta
    ratio = 1.0 / sigma
    steps = []
    for _ in range(SWEEPS):
        following = 1.0 / (2.0 * sigma - ratio)
        steps.append((following * ratio, 2.0 * following / delta))
        ratio = following
    return theta, steps


def chebyshev_terms():
    theta, steps = chebyshev_factors()
    terms = []
    before = None
    for keep, gain in steps:
        own, last = keep - gain * theta, 0.0
        if before is None:
            own += gain * theta
        else:
            own += gain / before[1]
            last = -gain / before[1] * before[0]
        terms.append((own, last, gain * filter_weight))
        before = keep, gain
    return theta, terms


def lanes(shape):
    return lax.broadcasted_iota(jnp.int32, shape, len(shape) - 1)


def lane_up(x):
    return jnp.where(lanes(x.shape) == A - 1, 0.0, pltpu.roll(x, A - 1, x.ndim - 1))


def lane_down(x):
    return jnp.where(lanes(x.shape) == 0, 0.0, pltpu.roll(x, 1, x.ndim - 1))


def fold_pack(halves):
    wide = halves[0].shape[0]
    lane = lanes((wide, A))
    packed = jnp.zeros((wide, A), jnp.float32)
    for row in range(R):
        at = W * (row % 4)
        for start, column in ((4 * row, 0), (64 + 4 * row, W - 4)):
            moved = turned(halves[row // 4], start - at - column)
            packed = jnp.where((lane >= start) & (lane < start + 4), moved, packed)
    if wide != 16:
        return packed
    lane = lanes((8, A))
    return jnp.where((lane & 32) == 0, packed[0:8], turned(packed[8:16], 32))


def unfolded(pack, steps):
    if pack.shape[0] != 8:
        return turned(pack, steps)
    return jnp.concatenate([turned(pack, steps), turned(pack, steps - 32)], axis=0)


def turned(x, steps):
    steps %= A
    return pltpu.roll(x, steps, 1) if steps else x


def edge_pack(halves):
    lane = lanes(halves[0].shape)
    packed = jnp.zeros(halves[0].shape, jnp.float32)
    for row in range(R):
        at = W * (row % 4)
        for start, column in ((8 * row, 0), (64 + 8 * row, W - 8)):
            moved = turned(halves[row // 4], start - at - column)
            packed = jnp.where((lane >= start) & (lane < start + 8), moved, packed)
    return packed


def peers_of(count):
    side = 4 if count == 16 else count
    steps = [(a, b) for a in range(count // side) for b in range(side)][1:]

    def hops(step):
        return min(step[0], count // side - step[0]) + min(step[1], side - step[1])

    return side, sorted(steps, key=hops, reverse=True)


def total(values):
    result = values[0]
    for value in values[1:]:
        result = result + value
    return result


def groups():
    return [
        ([(0, 1, 0, 0), (1, 0, 1, 0), (2, 0, 0, 1)], lame / 16, 2 * shear / 16),
        ([(0, 0, 1, 0), (1, 1, 0, 0)], shear / 16, None),
        ([(0, 0, 0, 1), (2, 1, 0, 0)], shear / 16, None),
        ([(1, 0, 0, 1), (2, 0, 1, 0)], shear / 16, None),
        ([(0, 0, 1, 1), (1, 1, 0, 1), (2, 1, 1, 0)], shear / 48, shear / 48),
        ([(0, 1, 0, 1), (1, 0, 1, 1)], lame / 48, 3 * shear / 48),
        ([(0, 1, 1, 0), (2, 0, 1, 1)], lame / 48, 3 * shear / 48),
        ([(1, 1, 1, 0), (2, 1, 0, 1)], lame / 48, 3 * shear / 48),
        ([(0, 1, 1, 1)], None, (lame + 4 * shear) / 144),
        ([(1, 1, 1, 1)], None, (lame + 4 * shear) / 144),
        ([(2, 1, 1, 1)], None, (lame + 4 * shear) / 144),
    ]


def element_forces(coefs, modulus):
    scaled = {}

    def times(weight, value):
        if weight not in scaled:
            scaled[weight] = modulus * weight
        return scaled[weight] * value

    forces = {}
    for members, joint, single in groups():
        if joint is not None:
            common = total([coefs[m] for m in members])
            if joint == single:
                for m in members:
                    forces[m] = times(joint, common + coefs[m])
                continue
            common = times(joint, common)
            for m in members:
                forces[m] = common if single is None else common + times(single, coefs[m])
        else:
            for m in members:
                forces[m] = times(single, coefs[m])
    return forces


def element_energy(coefs):
    terms = {}
    for members, joint, single in groups():
        if joint is not None:
            common = total([coefs[m] for m in members])
            terms.setdefault(joint, []).append(common * common)
        if single is not None:
            for m in members:
                terms.setdefault(single, []).append(coefs[m] * coefs[m])
    return total([weight * total(values) for weight, values in terms.items()])


def plane_sums(field, lifted, row, column):
    out = {}
    for c in range(3):
        near = field[c, row, pl.ds(column, 8), :]
        far = field[c, row, pl.ds(column + 1, 8), :]
        near_up = lifted[c, row, pl.ds(column, 8), :]
        far_up = lifted[c, row, pl.ds(column + 1, 8), :]
        for q, value, up in ((0, near + far, near_up + far_up), (1, far - near, far_up - near_up)):
            out[c, q, 0] = value + up
            out[c, q, 1] = up - value
    return out


def in_groups(first, last, size, action, carry=0):
    trips = (last - first) // size

    def trip(index, carry):
        for at in range(size):
            carry = action(first + index * size + at, carry)
        return carry

    if trips > 1:
        carry = lax.fori_loop(0, trips, trip, carry)
        first += trips * size
    for row in range(first, last):
        carry = action(row, carry)
    return carry


KEYS = [(c, q, r) for c in range(3) for q in range(2) for r in range(2)]


def row_coefs(low, high):
    coefs = {}
    for c, q, r in KEYS:
        coefs[c, 0, q, r] = low[c, q, r] + high[c, q, r]
        coefs[c, 1, q, r] = high[c, q, r] - low[c, q, r]
    return coefs


def kernel(
    counts,
    depth,
    density_in,
    prior_in,
    support_in,
    nodes_in,
    forces_in,
    displacement,
    sensitivity,
    density,
    prior,
    support,
    load_nodes,
    load_forces,
    raw,
    own,
    tile,
    beside,
    packs,
    halo,
    halos,
    wave0,
    wave1,
    wave2,
    wave3,
    wave4,
    remain,
    result,
    rows_low,
    rows_high,
    fixed_low,
    fixed_high,
    send_low,
    send_high,
    columns_low,
    columns_high,
    corners_low,
    corners_high,
    field,
    near_part,
    far_part,
    modulus,
    free,
    step_size,
    force,
    spread,
    energy,
    shares,
    weights,
    share,
    share_pack,
    beside2,
    packs2,
    ring_wave0,
    ring_wave1,
    ring_wave2,
    ring_wave3,
    ring_wave4,
    lifted,
    near_upper,
    far_upper,
    mask,
    ring_mask,
    around_send,
    around_recv,
    own_send,
    own_recv,
    halo_send,
    halo_recv,
    rows_send,
    rows_recv,
    column_send,
    column_recv,
    corner_send,
    corner_recv,
    share_send,
    share_recv,
    last_send,
    last_recv,
    fetched,
):
    n_load, n_x, n_y = counts
    waves = [wave0, wave1, wave2, wave3, wave4]
    wave = wave0
    ring_waves = [ring_wave0, ring_wave1, ring_wave2, ring_wave3, ring_wave4]
    wide = depth + 8
    load, gx, gy = lax.axis_index("load"), lax.axis_index("gx"), lax.axis_index("gy")

    def inside(dx, dy):
        return (gx + dx >= 0) & (gx + dx < n_x) & (gy + dy >= 0) & (gy + dy < n_y)

    side, steps = peers_of(n_load)

    def peer(step):
        a, b = steps[step]
        across = lax.rem(lax.div(load, side) + a, n_load // side)
        return across * side + lax.rem(lax.rem(load, side) + b, side)

    def each_peer(action):
        for step in range(n_load - 1):
            action(step)

    def remote(src, dst, send, recv, where):
        return pltpu.make_async_remote_copy(
            src_ref=src,
            dst_ref=dst,
            send_sem=send,
            recv_sem=recv,
            device_id=where,
            device_id_type=MESH,
        )

    def toward(dx, dy):
        return (load, gx + dx, gy + dy)

    barrier = pltpu.get_barrier_semaphore()
    each_peer(
        lambda step: pl.semaphore_signal(
            barrier, inc=1, device_id=(peer(step), gx, gy), device_id_type=MESH
        )
    )
    expected = n_load - 1
    for dx, dy in AROUND:
        expected = expected + inside(dx, dy).astype(jnp.int32)

        @pl.when(inside(dx, dy))
        def _():
            pl.semaphore_signal(
                barrier, inc=1, device_id=toward(dx, dy), device_id_type=MESH
            )

    fetches = [
        pltpu.make_async_copy(source, target, fetched.at[index])
        for index, (source, target) in enumerate(
            (
                (density_in, density),
                (prior_in, prior),
                (support_in, support),
                (nodes_in, load_nodes),
                (forces_in, load_forces),
            )
        )
    ]
    for fetch in fetches:
        fetch.start()

    fetches[0].wait()
    for row in range(R):
        raw[row, :, 0:W] = density[row]
    halves = []
    for half in range(2):
        value = jnp.zeros((depth, A), jnp.float32)
        lane = lanes(value.shape)
        for row in range(4):
            moved = turned(raw[4 * half + row], W * row)
            value = jnp.where((lane >= W * row) & (lane < W * row + W), moved, value)
        halves.append(value)
        own[:, A * half : A * half + A] = value
        tile[load, :, A * half : A * half + A] = value
    own[:, 2 * A : 3 * A] = edge_pack(halves)

    fetches[1].wait()
    fetches[2].wait()

    for row in range(R):
        for c in range(3):
            send_low[11 * row + 3 * c : 11 * row + 3 * c + 3, :] = prior[0, c, row, 0:3, :]
            send_high[7 * row + 2 * c : 7 * row + 2 * c + 2, :] = prior[0, c, row, W - 2 : W, :]
        send_low[11 * row + 9 : 11 * row + 11, :] = support[row, 0:2, :].astype(jnp.float32)
        send_high[7 * row + 6 : 7 * row + 7, :] = support[row, W - 1 : W, :].astype(jnp.float32)

    pl.semaphore_wait(barrier, expected)

    def around(index, whole, narrow, send, recv, sources, pack):
        dx, dy = AROUND[index]
        if dy == 0:
            return remote(
                sources[(1 + dx) // 2], whole.at[(1 - dx) // 2], send.at[index], recv.at[index], toward(dx, dy)
            )
        return remote(
            pack, narrow.at[1 - dx, (1 - dy) // 2], send.at[index], recv.at[index], toward(dx, dy)
        )

    first_around = [
        around(
            index,
            beside,
            packs,
            around_send,
            around_recv,
            [own.at[:, pl.ds(0, 2 * A)]] * 2,
            own.at[:, pl.ds(2 * A, A)],
        )
        for index in range(8)
    ]
    opposite = [AROUND.index((-dx, -dy)) for dx, dy in AROUND]

    for index, (dx, dy) in enumerate(AROUND):

        @pl.when(inside(dx, dy))
        def _():
            first_around[index].start()

    def own_copy(step):
        return remote(
            own.at[:, pl.ds(0, 2 * A)],
            tile.at[load],
            own_send.at[step],
            own_recv.at[step],
            (peer(step), gx, gy),
        )

    each_peer(lambda step: own_copy(step).start())

    row_copies = [
        (-1, remote(prior_in.at[0, :, pl.ds(0, 3)], rows_high, rows_send.at[0], rows_recv.at[0], toward(-1, 0))),
        (-1, remote(support_in.at[pl.ds(0, 2)], fixed_high, rows_send.at[1], rows_recv.at[1], toward(-1, 0))),
        (1, remote(prior_in.at[0, :, pl.ds(R - 2, 2)], rows_low, rows_send.at[2], rows_recv.at[2], toward(1, 0))),
        (1, remote(support_in.at[pl.ds(R - 1, 1)], fixed_low, rows_send.at[3], rows_recv.at[3], toward(1, 0))),
    ]
    column_copies = [
        (-1, remote(send_low, columns_high, column_send.at[0], column_recv.at[0], toward(0, -1))),
        (1, remote(send_high, columns_low, column_send.at[1], column_recv.at[1], toward(0, 1))),
    ]
    for dy, copy in column_copies:
        pl.when(inside(0, dy))(copy.start)
    for dx, copy in row_copies:
        pl.when(inside(dx, 0))(copy.start)

    for index, (dx, dy) in enumerate(AROUND):

        @pl.when(jnp.logical_not(inside(dx, dy)))
        def _():
            if dy == 0:
                for ref in (beside, beside2):
                    ref[(dx + 1) // 2] = jnp.zeros(ref.shape[1:], jnp.float32)
            else:
                for ref in (packs, packs2):
                    ref[dx + 1, (dy + 1) // 2] = jnp.zeros(ref.shape[2:], jnp.float32)

    @pl.when(jnp.logical_not(inside(-1, 0)))
    def _():
        rows_low[...] = jnp.zeros(rows_low.shape, jnp.float32)
        fixed_low[...] = jnp.zeros(fixed_low.shape, jnp.int32)
        corners_low[0] = jnp.zeros(corners_low.shape[1:], jnp.float32)
        corners_high[0] = jnp.zeros(corners_high.shape[1:], jnp.float32)

    @pl.when(jnp.logical_not(inside(1, 0)))
    def _():
        rows_high[...] = jnp.zeros(rows_high.shape, jnp.float32)
        fixed_high[...] = jnp.zeros(fixed_high.shape, jnp.int32)
        corners_low[1] = jnp.zeros(corners_low.shape[1:], jnp.float32)
        corners_high[1] = jnp.zeros(corners_high.shape[1:], jnp.float32)

    @pl.when(jnp.logical_not(inside(0, -1)))
    def _():
        columns_low[...] = jnp.zeros(columns_low.shape, jnp.float32)

    @pl.when(jnp.logical_not(inside(0, 1)))
    def _():
        columns_high[...] = jnp.zeros(columns_high.shape, jnp.float32)


    def in_grid(row, columns):
        row, columns = row + gx * R, columns + gy * W
        return (row >= 0) & (row < n_x * R) & (columns >= 0) & (columns < n_y * W)

    def halo_copy(step, part):
        span = pl.ds(part * 3 * A, 3 * A)
        return remote(
            halo.at[:, span],
            halos.at[load, :, span],
            halo_send.at[part, step],
            halo_recv.at[part, step],
            (peer(step), gx, gy),
        )

    for index, (dx, dy) in enumerate(AROUND):
        if dy == 0:

            @pl.when(inside(dx, dy))
            def _():
                first_around[opposite[index]].wait_recv()

    lane = lanes((depth, A))
    halo[:, 0:A] = beside[0, :, A : 2 * A]
    halo[:, A : 2 * A] = beside[1, :, 0:A]
    halo[:, 2 * A : 3 * A] = jnp.where(lane < 64, beside[1, :, A : 2 * A], beside[0, :, 0:A])
    halos[load, :, 0 : 3 * A] = halo[:, 0 : 3 * A]
    each_peer(lambda step: halo_copy(step, 0).start())

    fetches[3].wait()
    fetches[4].wait()
    flat = load_nodes[...]
    column_bits = (n_y * W).bit_length() - 1
    node_row = lax.shift_right_logical(flat, 7 + column_bits) - gx * R + 1
    node_column = (lax.shift_right_logical(flat, 7) & (n_y * W - 1)) - gy * W + 2
    held = (node_row >= 0) & (node_row < 11) & (node_column >= 0) & (node_column < USED)
    spread[0:1, :] = jnp.where(held, node_row * USED + node_column, -1)
    spread[1:2, :] = flat & (A - 1)
    force[...] = jnp.zeros(force.shape, jnp.float32)

    def add_loads(index, carry):
        span = pl.ds(pl.multiple_of(index * CHUNK, CHUNK), CHUNK)
        place = spread[0:1, span]
        depth_of = spread[1:2, span]
        left = jnp.where(
            lax.broadcasted_iota(jnp.int32, (11 * USED, CHUNK), 0) == place, 1.0, 0.0
        ).astype(jnp.bfloat16)
        here = lax.broadcasted_iota(jnp.int32, (A, CHUNK), 0) == depth_of
        rest = [load_forces[c, :, span] for c in range(3)]
        for part in range(3):
            rights = []
            for c in range(3):
                rounded = rest[c].astype(jnp.bfloat16).astype(jnp.float32)
                rest[c] = rest[c] - rounded
                rights.append(jnp.where(here, rounded, 0.0).astype(jnp.bfloat16))
            force[...] += lax.dot_general(
                left,
                jnp.concatenate(rights, axis=0),
                (((1,), (1,)), ((), ())),
                preferred_element_type=jnp.float32,
            )
        return carry

    chunks = load_nodes.shape[1] // CHUNK
    lax.fori_loop(0, chunks // 2, add_loads, 0)

    for index, (dx, dy) in enumerate(AROUND):
        if dy != 0:

            @pl.when(inside(dx, dy))
            def _():
                first_around[opposite[index]].wait_recv()

    for index in range(3):
        at = (3 + index) * A
        halo[:, at : at + A] = jnp.where(lane < 64, packs[index, 1], packs[index, 0])
        halos[load, :, at : at + A] = halo[:, at : at + A]
    each_peer(lambda step: halo_copy(step, 1).start())

    for dy, copy in column_copies:
        other = column_copies[0][1] if dy == 1 else column_copies[1][1]
        pl.when(inside(0, dy))(other.wait_recv)
    corner_copies = []
    for dx in (-1, 1):
        for part, (source, target) in enumerate(
            ((columns_low, corners_low), (columns_high, corners_high))
        ):
            at = (dx + 1) + part
            corner_copies.append(
                (
                    dx,
                    remote(
                        source,
                        target.at[(1 - dx) // 2],
                        corner_send.at[at],
                        corner_recv.at[at],
                        toward(dx, 0),
                    ),
                )
            )
    for dx, copy in corner_copies:
        pl.when(inside(dx, 0))(copy.start)

    lax.fori_loop(chunks // 2, chunks, add_loads, 0)

    def set_mask(row, carry):
        columns = lax.broadcasted_iota(jnp.int32, (48, A), 0) - 8
        mask[row] = jnp.where(in_grid(row - 8, columns), 1.0, 0.0)
        return carry

    in_groups(3, 21, 3, set_mask)

    def set_ring_mask(row, carry):
        lane = lanes((wide, A))
        layer = lax.broadcasted_iota(jnp.int32, (wide, A), 0) - 4 + load * depth
        kept = in_grid(row - 4, lane - 4) & (layer >= 0) & (layer < A) & (lane < W + 8)
        ring_mask[row] = jnp.where(kept, 1.0, 0.0)
        return carry

    in_groups(1, 15, 7, set_ring_mask)

    for c in range(3):
        for row in range(R):
            field[c, row + 2, 2 : 2 + W, :] = prior[0, c, row]
    for row in range(R):
        free[row + 2, 2 : 2 + W, :] = support[row].astype(jnp.float32)

    for dx, copy in row_copies + corner_copies:
        opposite_copy = {
            id(a[1]): b[1]
            for pairs in (
                (row_copies[0], row_copies[2]),
                (row_copies[1], row_copies[3]),
                (corner_copies[0], corner_copies[2]),
                (corner_copies[1], corner_copies[3]),
            )
            for a, b in (pairs, pairs[::-1])
        }[id(copy)]
        pl.when(inside(dx, 0))(opposite_copy.wait_recv)

    for c in range(3):
        for row in range(2):
            field[c, row, 2 : 2 + W, :] = rows_low[c, row]
        for row in range(3):
            field[c, row + 10, 2 : 2 + W, :] = rows_high[c, row]
    free[1, 2 : 2 + W, :] = fixed_low[0].astype(jnp.float32)
    for row in range(2):
        free[row + 10, 2 : 2 + W, :] = fixed_high[row].astype(jnp.float32)
    for row in range(-2, R + 3):
        if row < 0:
            low, high, at = corners_low.at[0], corners_high.at[0], row + R
        elif row < R:
            low, high, at = columns_low, columns_high, row
        else:
            low, high, at = corners_low.at[1], corners_high.at[1], row - R
        for c in range(3):
            field[c, row + 2, 0:2, :] = low[7 * at + 2 * c : 7 * at + 2 * c + 2, :]
            field[c, row + 2, 2 + W : 5 + W, :] = high[11 * at + 3 * c : 11 * at + 3 * c + 3, :]
        free[row + 2, 1:2, :] = low[7 * at + 6 : 7 * at + 7, :]
        free[row + 2, 2 + W : 4 + W, :] = high[11 * at + 9 : 11 * at + 11, :]

    def set_free(row, carry):
        columns = lax.broadcasted_iota(jnp.int32, (PITCH, A), 0) - 2
        kept = in_grid(row - 2, columns) & (columns >= -1) & (columns <= W + 1)
        free[row] = jnp.where(kept & (free[row] == 0.0), 1.0, 0.0)
        return carry

    in_groups(1, 12, 4, set_free)

    def lift(row, carry):
        for c in range(3):
            lifted[c, row] = lane_up(field[c, row])
        return carry

    in_groups(0, ROWS, 4, lift)

    def place(block, pieces):
        value = block.T
        for start, rows, columns, row, column in pieces:
            part = value[start : start + rows * columns].reshape(rows, columns, A)
            wave[row + 8 : row + 8 + rows, column + 16 : column + 16 + columns, :] = part

    each_peer(lambda step: own_copy(step).wait_recv())
    for half in range(2):
        place(tile[:, :, A * half : A * half + A].reshape(A, A), [(0, 4, W, 4 * half, 0)])
    layout = [
        [(0, 4, W, -4, 0)],
        [(0, 4, W, 8, 0)],
        [(0, 2, W, 12, 0), (64, 2, W, -6, 0)],
    ] + [[(0, 8, 8, dx * R, W), (64, 8, 8, dx * R, -8)] for dx in (-1, 0, 1)]
    for index, pieces in enumerate(layout):
        if index % 3 == 0:
            each_peer(lambda step: halo_copy(step, index // 3).wait_recv())
        place(halos[:, :, A * index : A * index + A].reshape(A, A), pieces)

    theta, terms = chebyshev_terms()

    def start_filter(row, carry):
        wave[row, 8:56, :] = wave[row, 8:56, :] / theta
        return carry

    in_groups(2, 22, 20, start_filter)
    for sweep, (own_factor, last_factor, near_factor) in enumerate(terms):

        def one_row(row, carry, source=waves[sweep], target=waves[sweep + 1]):
            middle = source[row, 8:56, :]
            near = (
                source[row - 1, 8:56, :]
                + source[row + 1, 8:56, :]
                + source[row, 7:55, :]
                + source[row, 9:57, :]
                + lane_up(middle)
                + lane_down(middle)
            )
            direction = own_factor * middle + near_factor * near
            if sweep:
                direction = direction + last_factor * waves[sweep - 1][row, 8:56, :]
            target[row, 8:56, :] = direction * mask[row]
            return carry

        in_groups(3 + sweep, 21 - sweep, 18, one_row)

    def set_modulus(row, carry):
        filtered = total([ref[row + 6, 14 : 14 + USED, :] for ref in waves])
        result[row] = filtered
        columns = lax.broadcasted_iota(jnp.int32, (USED, A), 0) - 2
        modulus[row, 0:8, :] = jnp.zeros((8, A), jnp.float32)
        modulus[row, 8 : 8 + USED, :] = jnp.where(
            in_grid(row - 2, columns), modulus_floor + filtered * filtered, 0.0
        )
        return carry

    in_groups(0, 12, 12, set_modulus)
    for half in range(2):
        tall = result[2 + 4 * half : 6 + 4 * half, 2 : 2 + W, :].reshape(A, A)
        weights[4 : 4 + A, A * half : A * half + A] = tall.T
    weights[0:4, :] = jnp.zeros((4, 2 * A), jnp.float32)
    weights[4 + A : 8 + A, :] = jnp.zeros((4, 2 * A), jnp.float32)

    def set_step(row, carry):
        around_node = total(
            [modulus[row - 1 + p, 7 + q : 7 + q + USED, :] for p in range(2) for q in range(2)]
        )
        around_node = around_node + lane_down(around_node)
        step_size[row] = relax_factor / ((lame + 4 * shear) / 9 * around_node)
        return carry

    in_groups(1, 12, 11, set_step)

    for sweep in range(JACOBI):
        first, last = 1 + sweep, 12 - sweep
        for block in range(BLOCKS):

            def one_element_row(row, carry, column=8 * block):
                low, pending = carry
                low = dict(zip(KEYS, low))
                high = plane_sums(field, lifted, row + 1, column)
                forces = element_forces(
                    row_coefs(low, high), modulus[row, pl.ds(column + 8, 8), :]
                )
                node = {}
                following = []
                for at, (c, q, r) in enumerate(KEYS):
                    change = forces[c, 1, q, r]
                    if (c, 0, q, r) in forces:
                        same = forces[c, 0, q, r]
                        node[c, q, r] = pending[at] + (same - change)
                        following.append(same + change)
                    else:
                        node[c, q, r] = pending[at] - change
                        following.append(change)
                for c in range(3):
                    for sign, near_to, far_to in (
                        (-1, near_part, far_part),
                        (1, near_upper, far_upper),
                    ):
                        sums, changes = (
                            node[c, q, 0] + node[c, q, 1] if sign > 0 else node[c, q, 0] - node[c, q, 1]
                            for q in range(2)
                        )
                        near_to[c, row, pl.ds(column, 8), :] = sums - changes
                        far_to[c, row, pl.ds(column + 1, 8), :] = sums + changes
                return [high[key] for key in KEYS], following

            low = plane_sums(field, lifted, first - 1, 8 * block)
            nothing = [jnp.zeros((8, A), jnp.float32)] * len(KEYS)
            in_groups(
                first - 1,
                last,
                last - first + 1,
                one_element_row,
                ([low[key] for key in KEYS], nothing),
            )

        def one_node_row(row, carry):
            span = pl.ds(0, USED)
            rate = step_size[row]
            open_here = free[row, span, :] > 0.0
            for c in range(3):
                applied = near_part[c, row, span, :] + far_part[c, row, span, :]
                applied = applied + lane_down(near_upper[c, row, span, :] + far_upper[c, row, span, :])
                load_here = force[pl.ds(pl.multiple_of((row - 1) * USED, 8), USED), A * c : A * c + A]
                moved = field[c, row, span, :] + (load_here - applied) * rate
                moved = jnp.where(open_here, moved, 0.0)
                field[c, row, span, :] = moved
                lifted[c, row, span, :] = lane_up(moved)
            return carry

        in_groups(first, last, 4, one_node_row)

    for block in range(W // 8):

        def one_energy_row(row, low, column=8 * block + 2):
            high = plane_sums(field, lifted, row + 1, column)
            value = element_energy(row_coefs(dict(zip(KEYS, low)), high))
            remain[row, pl.ds(column - 2, 8), :] = value
            return [high[key] for key in KEYS]

        low = plane_sums(field, lifted, 2, 8 * block + 2)
        in_groups(2, 10, 8, one_energy_row, [low[key] for key in KEYS])
    for half in range(2):
        tall = remain[2 + 4 * half : 6 + 4 * half, 0:W, :].reshape(A, A)
        energy[4 : 4 + A, A * half : A * half + A] = tall.T
    energy[0:4, :] = jnp.zeros((4, 2 * A), jnp.float32)
    energy[4 + A : 8 + A, :] = jnp.zeros((4, 2 * A), jnp.float32)

    def slab(owner):
        return pl.ds(pl.multiple_of(owner * depth, 8), wide)

    def share_copy(step):
        return remote(
            energy.at[slab(peer(step)), :],
            shares.at[step],
            share_send.at[step],
            share_recv.at[step],
            (peer(step), gx, gy),
        )

    each_peer(lambda step: share_copy(step).start())
    for c in range(3):
        for row in range(R):
            displacement[0, c, row] = field[c, row + 2, 2 : 2 + W, :]

    scale = -(2.0 / n_load) * weights[slab(load), :]
    each_peer(lambda step: share_copy(step).wait_recv())
    value = energy[slab(load), :]
    for step in range(n_load - 1):
        value = value + shares[step]
    value = scale * value
    share[...] = value
    share_pack[...] = fold_pack([value[:, 0:A], value[:, A : 2 * A]])

    sides = [share.at[:, pl.ds(0, A)], share.at[:, pl.ds(A, A)]]
    last_around = [
        around(index, beside2, packs2, last_send, last_recv, sides, share_pack)
        for index in range(8)
    ]
    for index, (dx, dy) in enumerate(AROUND):

        @pl.when(inside(dx, dy))
        def _():
            last_around[index].start()

    for index, (dx, dy) in enumerate(AROUND):

        @pl.when(inside(dx, dy))
        def _():
            last_around[opposite[index]].wait_recv()

    lane = lanes((wide, A))
    for row in range(-4, R + 4):
        if row < 0:
            body, pack = beside2[0], 0
        elif row < R:
            body, pack = share[:, A * (row // 4) : A * (row // 4) + A], 1
        else:
            body, pack = beside2[1], 2
        at = row % R
        line = turned(body, 4 - W * (at % 4))
        after = unfolded(packs2[pack, 1], 4 + W - 4 * at)
        before = unfolded(packs2[pack, 0], -64 - 4 * at)
        line = jnp.where(lane < 4, before, line)
        line = jnp.where(lane >= W + 4, after, line)
        line = jnp.where(lane < W + 8, line, 0.0)
        ring_waves[0][row + 4, 8 : 8 + wide, :] = line / theta

    span = slice(8, 8 + wide)
    for sweep, (own_factor, last_factor, near_factor) in enumerate(terms):
        source = ring_waves[sweep]
        for row in range(1 + sweep, 15 - sweep):
            middle = source[row, span, :]
            near = (
                source[row - 1, span, :]
                + source[row + 1, span, :]
                + source[row, 7 : 7 + wide, :]
                + source[row, 9 : 9 + wide, :]
                + pltpu.roll(middle, A - 1, 1)
                + pltpu.roll(middle, 1, 1)
            )
            direction = own_factor * middle + near_factor * near
            if sweep:
                direction = direction + last_factor * ring_waves[sweep - 1][row, span, :]
            ring_waves[sweep + 1][row, span, :] = direction * ring_mask[row]
    for row in range(R):
        summed = total([ref[row + 4, 12 : 12 + depth, :] for ref in ring_waves])
        sensitivity[row] = turned(summed, -4)[:, 0:W]

    for index, (dx, dy) in enumerate(AROUND):

        @pl.when(inside(dx, dy))
        def _():
            first_around[index].wait_send()
            last_around[index].wait_send()

    for dx, copy in row_copies + corner_copies:
        pl.when(inside(dx, 0))(copy.wait_send)
    for dy, copy in column_copies:
        pl.when(inside(0, dy))(copy.wait_send)
    each_peer(lambda step: own_copy(step).wait_send())
    each_peer(lambda step: halo_copy(step, 0).wait_send())
    each_peer(lambda step: halo_copy(step, 1).wait_send())
    each_peer(lambda step: share_copy(step).wait_send())


def body(counts, density, displacement_prior, support, load_nodes, load_forces):
    n_load = counts[0]
    depth = A // n_load
    wide = depth + 8
    folded = 8 if wide == 16 else wide
    picks = load_nodes.shape[1]
    real, whole = jnp.float32, jnp.int32
    scratch = [
        ((R, depth, W), real),
        (displacement_prior.shape, real),
        ((R, W, A), whole),
        ((1, picks), whole),
        ((3, 1, picks), real),
        ((R, depth, A), real),
        ((depth, 3 * A), real),
        ((n_load, depth, 2 * A), real),
        ((2, depth, 2 * A), real),
        ((3, 2, depth, A), real),
        ((depth, 6 * A), real),
        ((n_load, depth, 6 * A), real),
        ((24, 64, A), real),
        ((24, 64, A), real),
        ((24, 64, A), real),
        ((24, 64, A), real),
        ((24, 64, A), real),
        ((24, 48, A), real),
        ((12, USED, A), real),
        ((3, 2, W, A), real),
        ((3, 3, W, A), real),
        ((1, W, A), whole),
        ((2, W, A), whole),
        ((11 * R, A), real),
        ((7 * R, A), real),
        ((7 * R, A), real),
        ((11 * R, A), real),
        ((2, 7 * R, A), real),
        ((2, 11 * R, A), real),
        ((3, ROWS, PITCH, A), real),
        ((3, ROWS, PITCH, A), real),
        ((3, ROWS, PITCH, A), real),
        ((12, 8 + USED, A), real),
        ((ROWS, PITCH, A), real),
        ((12, USED, A), real),
        ((11 * USED, 3 * A), real),
        ((8, picks), whole),
        ((A + 8, 2 * A), real),
        ((n_load, wide, 2 * A), real),
        ((A + 8, 2 * A), real),
        ((wide, 2 * A), real),
        ((folded, A), real),
        ((2, wide, A), real),
        ((3, 2, folded, A), real),
        ((16, wide + 16, A), real),
        ((16, wide + 16, A), real),
        ((16, wide + 16, A), real),
        ((16, wide + 16, A), real),
        ((16, wide + 16, A), real),
        ((3, ROWS, PITCH, A), real),
        ((3, ROWS, PITCH, A), real),
        ((3, ROWS, PITCH, A), real),
        ((24, 48, A), real),
        ((16, wide, A), real),
    ]
    semaphores = [8, 8, n_load, n_load, (2, n_load), (2, n_load), 4, 4, 2, 2, 4, 4, n_load, n_load, 8, 8, 5]
    displacement, sensitivity = pl.pallas_call(
        functools.partial(kernel, counts, depth),
        out_shape=(
            pltpu.VMEM(displacement_prior.shape, real),
            pltpu.VMEM((R, depth, W), real),
        ),
        in_specs=[pl.BlockSpec(memory_space=pltpu.HBM)] * 5,
        out_specs=(pl.BlockSpec(memory_space=pltpu.VMEM),) * 2,
        scratch_shapes=[pltpu.VMEM(shape, kind) for shape, kind in scratch]
        + [pltpu.SemaphoreType.DMA(count if isinstance(count, tuple) else (count,)) for count in semaphores],
        compiler_params=pltpu.CompilerParams(
            collective_id=0, has_side_effects=True, vmem_limit_bytes=67_043_328 - (1 << 19),
        ),
        name="elasticity",
    )(
        jnp.transpose(density, (0, 2, 1)),
        displacement_prior,
        support,
        load_nodes,
        jnp.transpose(load_forces, (1, 0, 2)),
    )
    return displacement, jnp.transpose(sensitivity, (0, 2, 1))


def solution(mesh):
    counts = tuple(mesh.shape[axis] for axis in ("load", "gx", "gy"))
    return jax.shard_map(
        functools.partial(body, counts),
        mesh=mesh,
        in_specs=(
            P("gx", "gy", "load"),
            P("load", None, "gx", "gy", None),
            P("gx", "gy", None),
            P("load", None),
            P("load", None, None),
        ),
        out_specs=(P("load", None, "gx", "gy", None), P("gx", "gy", "load")),
        check_vma=False,
    )
```
